512 devices in a mesh: dom: 32 (over x, y, core), edge: 16 (over z).
Axes of the slice: x: 4, y: 4, z: 16, core: 2. Of those that a mesh axis runs over, the one named last changes fastest.
Arguments:
- edges: bfloat16 [524288, 512], P(('dom', 'edge')), may hold values from -6 to 6
- atoms: bfloat16 [16384, 256], P(('dom', 'edge')), may hold values from -6 to 6
- reverse: int32 [524288], P(('dom', 'edge')), may hold values from 0 to 524287, as said below
- atom_index: int32 [2, 524288], P(None, ('dom', 'edge')), may hold values from 0 to 511
- tile_source: int32 [8192, 2], P(('dom', 'edge')), may hold values from 0 to 255
- tiles: bfloat16 [8192, 64, 128], P(('dom', 'edge')), may hold values from -1 to 1
- weight_edge: bfloat16 [512, 512], replicated, may hold values from -0.25 to 0.25
- weight_down: bfloat16 [64, 512], replicated, may hold values from -0.25 to 0.25
- weight_up: bfloat16 [2, 64, 512], replicated, may hold values from -0.75 to 0.75
- weight_residual: bfloat16 [1, 2, 512, 512], replicated, may hold values from -0.25 to 0.25
- weight_message: bfloat16 [512, 256], replicated, may hold values from -0.25 to 0.25
- weight_atom: bfloat16 [2, 256, 256], replicated, may hold values from -0.375 to 0.375
- weight_join: bfloat16 [1024, 512], replicated, may hold values from -0.1875 to 0.1875
Outputs:
- new_edges: bfloat16 [524288, 512], P(('dom', 'edge'))
- new_atoms: bfloat16 [16384, 256], P(('dom', 'edge'))
The draws below stay inside these ranges and needn't reach their ends.
Inputs may be any that keep to these rules, and one draw needn't show every extreme that they name: reverse is an involution without fixed points. The reverse of a row lies on a device of the same edge index. Besides its own partition, the rows of each partition have their reverses in exactly 16 other partitions; at most 32 rows of one device have their reverses in any one other partition, and some device reaches 32.
All inputs are finite; a program needn't handle non-finite values.
Results may differ from the reference program's by a relative error of at most 0.015.
Values may be sent and summed in bfloat16 or wider, within the bound.
A program may use at most 64 MiB of HBM per device.

```python
import jax
import jax.numpy as jnp

D = 512
DA = 256
TR = 64
BLK = 64
K = 2
EPA = 32
NRES = 1
E_DEV = 1024
NNB = 16
CAP = 32
A_PART = 512
ATOMS = 16384
TOTAL_E = 524288
NB_PART = 256
NB_TOTAL = 8192
N_DOM = 32
N_EDGE = 16


def draw_reverse(key, part):
    key_list = jax.random.split(jax.random.fold_in(key, 11), 4)
    relabel = jax.random.permutation(key_list[0], N_DOM).astype(jnp.int32)
    inverse = jnp.argsort(relabel).astype(jnp.int32)
    totals = 2 * jax.random.permutation(key_list[1], N_DOM // 2)[:NNB].astype(jnp.int32) + 1
    partner = inverse[(totals[None, :] - relabel[:, None]) % N_DOM]
    lesser = jnp.minimum(jnp.arange(N_DOM, dtype=jnp.int32)[:, None], partner)
    count_table = 2 * jax.random.randint(key_list[2], (NNB, N_DOM, N_EDGE), 3 * CAP // 8, CAP // 2 + 1, dtype=jnp.int32)
    count_table = count_table.at[0, 0, 0].set(CAP)
    counts = count_table[jnp.arange(NNB, dtype=jnp.int32)[None, :], lesser, :]
    canonical = jnp.arange(E_DEV, dtype=jnp.int32)
    region = canonical // CAP
    within = canonical % CAP
    region_cap = jnp.minimum(region, NNB - 1)
    domain_ids = jnp.arange(N_DOM, dtype=jnp.int32)[:, None, None]
    edge_ids = jnp.arange(N_EDGE, dtype=jnp.int32)[None, :, None]
    limits = counts[domain_ids, region_cap[None, None, :], edge_ids]
    is_cross = (region[None, None, :] < NNB) & (within[None, None, :] < limits)
    far_domain = partner[domain_ids, region_cap[None, None, :]]
    target_dom = jnp.where(is_cross, far_domain, domain_ids)
    target_canon = jnp.where(is_cross, canonical[None, None, :], jnp.bitwise_xor(canonical, 1)[None, None, :])
    device_keys = jax.random.split(key_list[3], N_DOM * N_EDGE)
    shuffle = jax.vmap(lambda single: jax.random.permutation(single, E_DEV))(device_keys).astype(jnp.int32)
    shuffle = shuffle.reshape(N_DOM, N_EDGE, E_DEV)
    unshuffle = jnp.argsort(shuffle, axis=-1).astype(jnp.int32)
    target_edge = jnp.broadcast_to(edge_ids, target_dom.shape)
    target_pos = shuffle[target_dom, target_edge, target_canon]
    target_global = (target_dom * N_EDGE + target_edge) * E_DEV + target_pos
    result = jnp.take_along_axis(target_global, unshuffle, axis=-1)
    return result.reshape(-1).astype(jnp.int32)


def with_ends(array, key, low, largest):
    longest = array.shape.index(max(array.shape))
    spots = []
    for shift in (0, 1):
        where = [jax.random.randint(jax.random.fold_in(key, axis), (), 0, length) for axis, length in enumerate(array.shape)]
        where[longest] = (where[longest] + shift) % array.shape[longest]
        spots.append(tuple(where))
    return array.at[spots[0]].set(low).at[spots[1]].set(largest)


def block_levels(key, dims, pieces, least, high):
    level, own = 1.0, jax.random.fold_in(key, 6)
    for axis_at, blocks in pieces:
        steps = jnp.exp(jax.random.uniform(jax.random.fold_in(own, axis_at), (blocks,), jnp.float32, least / len(pieces), high / len(pieces)))
        level = level * jnp.repeat(steps, dims[axis_at] // blocks).reshape([-1 if axis == axis_at else 1 for axis in range(len(dims))])
    return level


def noise(stream_key, extent, deviation, most, cuts=(), kind=jnp.bfloat16):
    drawn = jax.random.normal(stream_key, extent, jnp.float32) * deviation
    if len(cuts) > 0:
        drawn = block_levels(stream_key, extent, cuts, -0.22, 0.18) * drawn
    return jnp.clip(drawn, min=-most, max=most).astype(kind)


def setup_inputs(seed: int = 0) -> dict:
    streams_of = jax.random.split(jax.random.key(seed), 14)
    return {
        "edges": noise(streams_of[0], (TOTAL_E, D), 1.0, 6.0, ((0, 512),)),
        "atoms": noise(streams_of[1], (ATOMS, DA), 1.0, 6.0, ((0, 512),)),
        "reverse": draw_reverse(jax.random.fold_in(streams_of[13], 71), 0),
        "atom_index": with_ends(jax.random.randint(streams_of[3], (2, TOTAL_E), 0, A_PART), jax.random.fold_in(streams_of[3], 1), 0, A_PART - 1).astype(jnp.int32),
        "tile_source": with_ends(jax.random.randint(streams_of[4], (NB_TOTAL, K), 0, NB_PART), jax.random.fold_in(streams_of[4], 1), 0, NB_PART - 1).astype(jnp.int32),
        "tiles": noise(streams_of[5], (NB_TOTAL, BLK, K * BLK), (K * BLK // 4) ** -0.5, 1.0, ((0, 512),)),
        "weight_edge": noise(streams_of[6], (D, D), D ** -0.5, 0.25),
        "weight_down": noise(streams_of[7], (TR, D), D ** -0.5, 0.25),
        "weight_up": noise(streams_of[8], (2, TR, D), TR ** -0.5, 0.75),
        "weight_residual": noise(streams_of[9], (NRES, 2, D, D), D ** -0.5, 0.25),
        "weight_message": noise(streams_of[10], (D, DA), D ** -0.5, 0.25),
        "weight_atom": noise(streams_of[11], (2, DA, DA), DA ** -0.5, 0.375),
        "weight_join": noise(streams_of[12], (2 * DA + D, D), (2 * DA + D) ** -0.5, 0.1875),
    }


root_half = 0.7071067811865476


def reference(edges, atoms, reverse, atom_index, tile_source, tiles, weight_edge, weight_down, weight_up, weight_residual, weight_message, weight_atom, weight_join):
    hidden = jax.nn.silu(jnp.dot(edges, weight_edge, preferred_element_type=jnp.float32)).astype(jnp.bfloat16)
    narrow = jax.nn.silu(jnp.dot(hidden, weight_down.T, preferred_element_type=jnp.float32)).astype(jnp.bfloat16)
    blocks = narrow.reshape(NB_TOTAL, BLK, TR)
    owners = (jnp.arange(NB_TOTAL, dtype=jnp.int32) // NB_PART) * NB_PART
    source = owners[:, None] + tile_source
    picked = blocks[source].astype(jnp.float32)
    shaped = tiles.reshape(NB_TOTAL, BLK, K, BLK).astype(jnp.float32)
    mixed = jnp.einsum("bekj,bkjt->bet", shaped, picked)
    trip_out = mixed.reshape(TOTAL_E, TR).astype(jnp.bfloat16)
    swapped = jnp.dot(trip_out, weight_up[1], preferred_element_type=jnp.float32).astype(jnp.bfloat16)
    direct = jnp.dot(trip_out, weight_up[0], preferred_element_type=jnp.float32)
    joined = (direct + swapped[reverse].astype(jnp.float32)) * root_half
    edge_state = (edges.astype(jnp.float32) + joined).astype(jnp.bfloat16)
    for layer_index in range(NRES):
        middle = jax.nn.silu(jnp.dot(edge_state, weight_residual[layer_index, 0], preferred_element_type=jnp.float32)).astype(jnp.bfloat16)
        branch = jax.nn.silu(jnp.dot(middle, weight_residual[layer_index, 1], preferred_element_type=jnp.float32))
        edge_state = ((edge_state.astype(jnp.float32) + branch) * root_half).astype(jnp.bfloat16)
    message = jnp.dot(edge_state, weight_message, preferred_element_type=jnp.float32).astype(jnp.bfloat16)
    partition = jnp.arange(TOTAL_E, dtype=jnp.int32) // (E_DEV * N_EDGE)
    target = partition * A_PART + atom_index[1]
    source_atom = partition * A_PART + atom_index[0]
    atom_sums = jax.ops.segment_sum(message.astype(jnp.float32), target, num_segments=ATOMS)
    scaled = (atom_sums * (EPA ** -0.5)).astype(jnp.bfloat16)
    atom_middle = jax.nn.silu(jnp.dot(scaled, weight_atom[0], preferred_element_type=jnp.float32)).astype(jnp.bfloat16)
    new_atoms = (atoms.astype(jnp.float32) + jnp.dot(atom_middle, weight_atom[1], preferred_element_type=jnp.float32)).astype(jnp.bfloat16)
    gathered = jnp.concatenate([new_atoms[source_atom], new_atoms[target], edge_state], axis=1)
    update = jax.nn.silu(jnp.dot(gathered, weight_join, preferred_element_type=jnp.float32))
    new_edges = ((edge_state.astype(jnp.float32) + update) * root_half).astype(jnp.bfloat16)
    return new_edges, new_atoms
```

```python
import functools

import jax
import jax.numpy as jnp
from jax import lax
from jax.experimental import pallas as pl
from jax.experimental.pallas import tpu as pltpu
from jax.sharding import PartitionSpec as P

EPA = 32
ROOT_HALF = 0.7071067811865476
MESH = pl.DeviceIdType.MESH
BF16 = jnp.bfloat16
F32 = jnp.float32
I32 = jnp.int32
CHUNKS = 4
PIECES = 8


def silu(v):
    half = 0.5 * v
    return half + half * jnp.tanh(half)


def dot(a, b):
    return jnp.dot(a, b, preferred_element_type=F32)


def dot_nt(a, b):
    return lax.dot_general(a, b, (((1,), (1,)), ((), ())), preferred_element_type=F32)


def iota(shape, axis):
    return lax.broadcasted_iota(I32, shape, axis)


def log2(n):
    assert n & (n - 1) == 0
    return n.bit_length() - 1


def flag(cond):
    return jnp.where(cond, jnp.float32(1), jnp.float32(0))


def kernel(
    n_dom,
    n_edge,
    ts_ref,
    rev_ref,
    ai_ref,
    atoms_ref,
    wd_ref,
    edges_h,
    tiles_h,
    we_h,
    wup_h,
    wres_h,
    wmsg_h,
    watom_h,
    wjoin_h,
    out_ref,
    natoms_ref,
    edges_v,
    tiles_v,
    we_v,
    wup_v,
    wres_v,
    wmsg_v,
    watom_v,
    wjoin_v,
    gath,
    trip_v,
    pack_v,
    arr_v,
    mir_v,
    sel_v,
    loc_v,
    rec_v,
    keep_v,
    tgt_t,
    src_g,
    tgt_g,
    cols_v,
    rank_v,
    es_v,
    msg_v,
    pre_v,
    rs_v,
    rr_v,
    na_v,
    load_sem,
    ring_send,
    ring_recv,
    x_sem,
    z_sem,
):
    me_d = lax.axis_index("dom")
    me_z = lax.axis_index("edge")
    rows, width = edges_v.shape
    groups = gath.shape[0] // n_edge
    part_atoms, atom_width = rs_v.shape
    own_atoms = part_atoms // n_edge
    half_cap = pack_v.shape[0] // n_dom
    slots = pack_v.shape[0]
    steps = n_edge // 2
    per = groups // CHUNKS
    edge_half = rows // 2
    sub = edge_half // CHUNKS
    right = lax.rem(me_z + 1, n_edge)
    left = lax.rem(me_z + n_edge - 1, n_edge)

    def load(i, src, dst):
        return pltpu.make_async_copy(src, dst, load_sem.at[i])

    edge_loads = [
        [
            load(2 * c + h, edges_h.at[pl.ds(h * edge_half + c * sub, sub)], edges_v.at[pl.ds(h * edge_half + c * sub, sub)])
            for h in range(2)
        ]
        for c in range(CHUNKS)
    ]
    base = 2 * CHUNKS
    we_load = load(base, we_h, we_v)
    others = [
        load(base + 1, tiles_h, tiles_v),
        load(base + 2, wup_h, wup_v),
        load(base + 3, wres_h, wres_v),
        load(base + 4, wmsg_h, wmsg_v),
        load(base + 5, watom_h, watom_v),
        load(base + 6, wjoin_h, wjoin_v),
    ]
    we_load.start()
    for pair in edge_loads:
        for one in pair:
            one.start()

    barrier = pltpu.get_barrier_semaphore()
    for peer in (left, right):
        pl.semaphore_signal(barrier, inc=1, device_id={"edge": peer}, device_id_type=MESH)

    def greet(k, carry):
        pl.semaphore_signal(
            barrier, inc=1, device_id={"dom": lax.rem(me_d + k, n_dom)}, device_id_type=MESH
        )
        return carry

    lax.fori_loop(1, n_dom, greet, 0)
    for one in others:
        one.start()

    def ring(direction, s, c, receiving):
        if direction == 0:
            slot = lax.rem(me_z - s - (1 if receiving else 0) + 2 * n_edge, n_edge)
            to = right
        else:
            slot = lax.rem(me_z + s + (1 if receiving else 0), n_edge)
            to = left
        view = gath.at[pl.ds(slot * groups + c * per, per)]
        return pltpu.make_async_remote_copy(
            src_ref=view,
            dst_ref=view,
            send_sem=ring_send.at[direction, s, c],
            recv_sem=ring_recv.at[direction, s, c],
            device_id={"edge": to},
            device_id_type=MESH,
        )

    zeros_down = jnp.zeros_like(wd_ref[...])
    wd_lo = jnp.concatenate([wd_ref[...], zeros_down], axis=0)
    wd_hi = jnp.concatenate([zeros_down, wd_ref[...]], axis=0)
    we_load.wait()
    for c in range(CHUNKS):
        for one in edge_loads[c]:
            one.wait()
        x = jnp.concatenate(
            [edges_v[pl.ds(c * sub, sub)], edges_v[pl.ds(edge_half + c * sub, sub)]], axis=0
        )
        hidden = silu(dot(x, we_v[...])).astype(BF16)
        narrow = silu(dot_nt(hidden[:sub], wd_lo) + dot_nt(hidden[sub:], wd_hi)).astype(BF16)
        gath[pl.ds(me_z * groups + c * per, per)] = narrow.reshape(per, narrow.shape[0] // per, narrow.shape[1])
        if c == 0:
            pl.semaphore_wait(barrier, n_dom + 1)
        ring(0, 0, c, False).start()
        ring(1, 0, c, False).start()

    shift = log2(rows * n_edge)
    rev_row = rev_ref[...]
    hold_row = lax.shift_right_logical(rev_row, shift)
    local_row = hold_row == me_d
    src_row = rev_row & (rows - 1)
    for i, row in enumerate((rev_row, ai_ref[0:1], ai_ref[1:2])):
        cols_v[i] = jnp.transpose(jnp.broadcast_to(row.astype(F32), (8, rows))).astype(I32)
    piece = rows // PIECES

    def forward(t):
        s, c = 1 + lax.div(t, CHUNKS), lax.rem(t, CHUNKS)
        for direction in range(2):
            ring(direction, s - 1, c, True).wait_recv()
            ring(direction, s, c, False).start()

    def ranks(i):
        at = i * piece
        here = pl.ds(at, piece)
        rev_col = cols_v[0, here, 0:1]
        hold_col = lax.shift_right_logical(rev_col, shift)
        before = (hold_col == hold_row) & (iota((piece, rows), 0) + at < iota((piece, rows), 1))
        rank_v[...] = rank_v[...] + jnp.sum(flag(before), axis=0, keepdims=True)
        lower = (rev_row >= lax.shift_left(hold_col, shift)) & (rev_row < rev_col)
        rank = jnp.sum(flag(lower), axis=1, keepdims=True).astype(I32)
        high = jnp.where(rank >= half_cap, 1, 0)
        code = jnp.where(hold_col == me_d, -1, hold_col * half_cap + rank - high * half_cap)
        rec_v[here] = flag(iota((piece, slots), 1) == code).astype(BF16)
        keep_v[here] = flag((iota((piece, 128), 1) >= 64) == (high == 1))

    def select(i):
        at = i * piece
        here = pl.ds(at, piece)
        rank = rank_v[0:1].astype(I32)
        high = jnp.where(rank >= half_cap, 1, 0)
        code = jnp.where(local_row, -1, hold_row * half_cap + rank + high * (slots - half_cap))
        at_slot = i * (2 * slots // PIECES)
        sel_v[pl.ds(at_slot, 2 * slots // PIECES)] = flag(
            iota((2 * slots // PIECES, rows), 0) + at_slot == code
        ).astype(BF16)
        rev_col = cols_v[0, here, 0:1]
        from_col = jnp.where(
            lax.shift_right_logical(rev_col, shift) == me_d, rev_col & (rows - 1), -1
        )
        loc_v[here] = flag(iota((piece, rows), 1) == from_col).astype(BF16)

    def onehots(i):
        here = pl.ds(i * piece, piece)
        atom_piece = part_atoms // PIECES
        tgt_t[pl.ds(i * atom_piece, atom_piece)] = flag(
            iota((atom_piece, rows), 0) + i * atom_piece == ai_ref[1:2]
        ).astype(BF16)
        lanes = iota((piece, part_atoms), 1)
        src_g[here] = flag(lanes == cols_v[1, here, 0:1]).astype(BF16)
        tgt_g[here] = flag(lanes == cols_v[2, here, 0:1]).astype(BF16)

    rank_v[...] = jnp.zeros_like(rank_v)
    middle = (steps - 2) * CHUNKS
    for k, work in enumerate((ranks, select, onehots)):

        def turn(i, carry, k=k, work=work):
            if k * PIECES < middle:
                forward(k * PIECES + i)
            work(i)
            return carry

        lax.fori_loop(0, PIECES, turn, 0)

    arr_v[pl.ds(me_d * half_cap, half_cap)] = jnp.zeros((half_cap, 128), BF16)

    last = steps - 1
    split = CHUNKS // 2
    for c in range(CHUNKS):
        for direction in range(2):
            ring(direction, last - 1, c, True).wait_recv()
            if (c < split) == (direction == 0):
                ring(direction, last, c, False).start()
    for c in range(CHUNKS):
        ring(0 if c < split else 1, last, c, True).wait_recv()

    others[0].wait()
    blocks = tiles_v.shape[0]
    lane_half = lax.shift_right_logical(iota((64, 128), 1), 6)
    for b in range(blocks):
        picked = []
        for k in range(2):
            source = ts_ref[b, k]
            owner = lax.shift_right_logical(source, log2(blocks))
            inner = source & (blocks - 1)
            value = gath[owner * groups + (inner & (groups - 1))]
            picked.append(
                jnp.where(lane_half == lax.shift_right_logical(inner, log2(groups)), value, jnp.zeros_like(value))
            )
        mixed = dot(tiles_v[b], jnp.concatenate(picked, axis=0))
        trip_v[pl.ds(b * 64, 64)] = (mixed + pltpu.roll(mixed, 64, 1)).astype(BF16)

    low_lanes = iota((slots, 128), 1) < 64
    pack_v[...] = jnp.where(
        low_lanes, dot(sel_v[pl.ds(0, slots)], trip_v[...]), dot(sel_v[pl.ds(slots, slots)], trip_v[...])
    ).astype(BF16)

    def send_dom(k, carry):
        peer = lax.rem(me_d + k, n_dom)
        pltpu.make_async_remote_copy(
            src_ref=pack_v.at[pl.ds(peer * half_cap, half_cap)],
            dst_ref=arr_v.at[pl.ds(me_d * half_cap, half_cap)],
            send_sem=x_sem.at[0],
            recv_sem=x_sem.at[1],
            device_id={"dom": peer},
            device_id_type=MESH,
        ).start()
        return carry

    lax.fori_loop(1, n_dom, send_dom, 0)
    all_but_one = pl.ds(0, slots - half_cap)
    exchange = pltpu.make_async_remote_copy(
        src_ref=pack_v.at[all_but_one],
        dst_ref=arr_v.at[all_but_one],
        send_sem=x_sem.at[0],
        recv_sem=x_sem.at[1],
        device_id={"dom": lax.rem(me_d + 1, n_dom)},
        device_id_type=MESH,
    )
    part = rows // 4
    for i in range(4):
        mir_v[pl.ds(i * part, part)] = dot(loc_v[pl.ds(i * part, part)], trip_v[...])
    for one in others[1:]:
        one.wait()
    exchange.wait()

    def edge_part(i, carry):
        here = pl.ds(i * part, part)
        found = dot(rec_v[here], arr_v[...]) * keep_v[here]
        mirrored = (found + pltpu.roll(found, 64, 1) + mir_v[here]).astype(BF16)
        both = jnp.where(iota((part, 128), 1) < 64, trip_v[here], mirrored)
        state = (edges_v[here].astype(F32) + dot(both, wup_v[...]) * ROOT_HALF).astype(BF16)
        middle = silu(dot(state, wres_v[0])).astype(BF16)
        branch = silu(dot(middle, wres_v[1]))
        state = ((state.astype(F32) + branch) * ROOT_HALF).astype(BF16)
        es_v[here] = state
        msg_v[here] = dot(state, wmsg_v[...]).astype(BF16)
        return carry

    lax.fori_loop(0, 4, edge_part, 0)

    a_part = part_atoms // 4
    for i in range(4):
        here = pl.ds(i * a_part, a_part)
        rs_v[here] = dot(tgt_t[here], msg_v[...]).astype(BF16)

    def send_sums(k, carry):
        peer = lax.rem(me_z + k, n_edge)
        pltpu.make_async_remote_copy(
            src_ref=rs_v.at[pl.ds(peer * own_atoms, own_atoms)],
            dst_ref=rr_v.at[pl.ds(me_z * own_atoms, own_atoms)],
            send_sem=z_sem.at[0],
            recv_sem=z_sem.at[1],
            device_id={"edge": peer},
            device_id_type=MESH,
        ).start()
        return carry

    lax.fori_loop(1, n_edge, send_sums, 0)
    own = pl.ds(me_z * own_atoms, own_atoms)
    rr_v[own] = rs_v[own]

    def pre_part(i, carry):
        here = pl.ds(i * part, part)
        pre_v[here] = dot(es_v[here], wjoin_v[pl.ds(2 * atom_width, width)])
        return carry

    lax.fori_loop(0, 4, pre_part, 0)
    most = pl.ds(0, part_atoms - own_atoms)
    sums = pltpu.make_async_remote_copy(
        src_ref=rs_v.at[most],
        dst_ref=rr_v.at[most],
        send_sem=z_sem.at[0],
        recv_sem=z_sem.at[1],
        device_id={"edge": right},
        device_id_type=MESH,
    )
    sums.wait()
    total = jnp.zeros((own_atoms, atom_width), F32)
    for j in range(n_edge):
        total = total + rr_v[pl.ds(j * own_atoms, own_atoms)].astype(F32)
    scaled = (total * EPA ** (-0.5)).astype(BF16)
    middle_atoms = silu(dot(scaled, watom_v[0])).astype(BF16)
    fresh = (atoms_ref[...].astype(F32) + dot(middle_atoms, watom_v[1])).astype(BF16)
    natoms_ref[...] = fresh
    na_v[own] = fresh

    def send_atoms(k, carry):
        peer = lax.rem(me_z + k, n_edge)
        pltpu.make_async_remote_copy(
            src_ref=na_v.at[own],
            dst_ref=na_v.at[own],
            send_sem=z_sem.at[2],
            recv_sem=z_sem.at[3],
            device_id={"edge": peer},
            device_id_type=MESH,
        ).start()
        return carry

    lax.fori_loop(1, n_edge, send_atoms, 0)
    pltpu.make_async_remote_copy(
        src_ref=na_v.at[most],
        dst_ref=na_v.at[most],
        send_sem=z_sem.at[2],
        recv_sem=z_sem.at[3],
        device_id={"edge": right},
        device_id_type=MESH,
    ).wait()

    def final_part(i, carry):
        here = pl.ds(i * part, part)
        ends = jnp.concatenate([dot(src_g[here], na_v[...]), dot(tgt_g[here], na_v[...])], axis=1).astype(BF16)
        update = silu(dot(ends, wjoin_v[pl.ds(0, 2 * atom_width)]) + pre_v[here])
        out_ref[here] = ((es_v[here].astype(F32) + update) * ROOT_HALF).astype(BF16)
        return carry

    lax.fori_loop(0, 4, final_part, 0)

    def drain(t, carry):
        s, c = lax.div(t, CHUNKS), lax.rem(t, CHUNKS)
        for direction in range(2):
            ring(direction, s, c, False).wait_send()
        return carry

    lax.fori_loop(0, last * CHUNKS, drain, 0)
    for c in range(CHUNKS):
        ring(0 if c < split else 1, last, c, False).wait_send()


def body(n_dom, n_edge, edges, atoms, reverse, atom_index, tile_source, tiles, weight_edge, weight_down, weight_up,
         weight_residual, weight_message, weight_atom, weight_join):
    rows, width = edges.shape
    own_atoms, atom_width = atoms.shape
    part_atoms = own_atoms * n_edge
    blocks = tiles.shape[0]
    channels = weight_down.shape[0]
    assert channels == 64 and tiles.shape[1:] == (64, 128)
    groups = blocks // 2
    capacity = rows // n_dom
    slots = n_dom * capacity // 2
    vmem = pl.BlockSpec(memory_space=pltpu.VMEM)
    hbm = pl.BlockSpec(memory_space=pl.ANY)
    return pl.pallas_call(
        functools.partial(kernel, n_dom, n_edge),
        out_shape=(
            jax.ShapeDtypeStruct((rows, width), BF16),
            jax.ShapeDtypeStruct((own_atoms, atom_width), BF16),
        ),
        in_specs=[pl.BlockSpec(memory_space=pltpu.SMEM)] + [vmem] * 4 + [hbm] * 8,
        out_specs=(vmem, vmem),
        scratch_shapes=[
            pltpu.VMEM((rows, width), BF16),
            pltpu.VMEM(tiles.shape, BF16),
            pltpu.VMEM(weight_edge.shape, BF16),
            pltpu.VMEM((2 * channels, width), BF16),
            pltpu.VMEM((2, width, width), BF16),
            pltpu.VMEM(weight_message.shape, BF16),
            pltpu.VMEM(weight_atom.shape, BF16),
            pltpu.VMEM(weight_join.shape, BF16),
            pltpu.VMEM((n_edge * groups, 64, 128), BF16),
            pltpu.VMEM((rows, 128), BF16),
            pltpu.VMEM((slots, 128), BF16),
            pltpu.VMEM((slots, 128), BF16),
            pltpu.VMEM((rows, 128), F32),
            pltpu.VMEM((2 * slots, rows), BF16),
            pltpu.VMEM((rows, rows), BF16),
            pltpu.VMEM((rows, slots), BF16),
            pltpu.VMEM((rows, 128), F32),
            pltpu.VMEM((part_atoms, rows), BF16),
            pltpu.VMEM((rows, part_atoms), BF16),
            pltpu.VMEM((rows, part_atoms), BF16),
            pltpu.VMEM((3, rows, 8), I32),
            pltpu.VMEM((8, rows), F32),
            pltpu.VMEM((rows, width), BF16),
            pltpu.VMEM((rows, atom_width), BF16),
            pltpu.VMEM((rows, width), F32),
            pltpu.VMEM((part_atoms, atom_width), BF16),
            pltpu.VMEM((part_atoms, atom_width), BF16),
            pltpu.VMEM((part_atoms, atom_width), BF16),
            pltpu.SemaphoreType.DMA((2 * CHUNKS + 7,)),
            pltpu.SemaphoreType.DMA((2, n_edge // 2, CHUNKS)),
            pltpu.SemaphoreType.DMA((2, n_edge // 2, CHUNKS)),
            pltpu.SemaphoreType.DMA((2,)),
            pltpu.SemaphoreType.DMA((4,)),
        ],
        compiler_params=pltpu.CompilerParams(
            collective_id=0, has_side_effects=True, vmem_limit_bytes=56 * 1024 * 1024
        ),
    )(
        tile_source,
        reverse.reshape(1, rows),
        atom_index,
        atoms,
        weight_down,
        edges,
        tiles,
        weight_edge,
        weight_up.reshape(2 * channels, width),
        weight_residual.reshape(2, width, width),
        weight_message,
        weight_atom,
        weight_join,
    )


def solution(mesh):
    n_dom, n_edge = mesh.shape["dom"], mesh.shape["edge"]
    placed = (
        P(("dom", "edge"), None),
        P(("dom", "edge"), None),
        P(("dom", "edge")),
        P(None, ("dom", "edge")),
        P(("dom", "edge"), None),
        P(("dom", "edge"), None, None),
        P(),
        P(),
        P(),
        P(),
        P(),
        P(),
        P(),
    )
    return jax.shard_map(
        functools.partial(body, n_dom, n_edge),
        mesh=mesh,
        in_specs=placed,
        out_specs=(P(("dom", "edge"), None), P(("dom", "edge"), None)),
        check_vma=False,
    )
```

```python
import functools

import jax
import jax.numpy as jnp
from jax import lax
from jax.experimental import pallas as pl
from jax.experimental.pallas import tpu as pltpu
from jax.sharding import PartitionSpec as P

EPA = 32
ROOT_HALF = 0.7071067811865476
MESH = pl.DeviceIdType.MESH
BF16 = jnp.bfloat16
F32 = jnp.float32
I32 = jnp.int32
CHUNKS = 8
PIECES = 16


def silu(v):
    half = 0.5 * v
    return half + half * jnp.tanh(half)


def dot(a, b):
    return jnp.dot(a, b, preferred_element_type=F32)


def dot_nt(a, b):
    return lax.dot_general(a, b, (((1,), (1,)), ((), ())), preferred_element_type=F32)


def iota(shape, axis):
    return lax.broadcasted_iota(I32, shape, axis)


def log2(n):
    assert n & (n - 1) == 0
    return n.bit_length() - 1


def flag(cond):
    return jnp.where(cond, jnp.float32(1), jnp.float32(0))


def kernel(
    n_dom,
    n_edge,
    ts_ref,
    rev_ref,
    ai_ref,
    atoms_ref,
    wd_ref,
    edges_h,
    tiles_h,
    we_h,
    wup_h,
    wres_h,
    wmsg_h,
    watom_h,
    wjoin_h,
    out_ref,
    natoms_ref,
    edges_v,
    tiles_v,
    we_v,
    wup_v,
    wres_v,
    wmsg_v,
    watom_v,
    wjoin_v,
    gath,
    trip_v,
    pack_v,
    arr_v,
    mir_v,
    sel_v,
    loc_v,
    rec_v,
    keep_v,
    tgt_t,
    src_g,
    tgt_g,
    cols_v,
    rank_v,
    es_v,
    msg_v,
    pre_v,
    rs_v,
    rel_v,
    hop_v,
    fin_v,
    na_v,
    load_sem,
    ring_send,
    ring_recv,
    x_sem,
    z_sem,
):
    me_d = lax.axis_index("dom")
    me_z = lax.axis_index("edge")
    rows, width = edges_v.shape
    groups = gath.shape[0] // n_edge
    part_atoms, atom_width = rs_v.shape
    own_atoms = part_atoms // n_edge
    half_cap = pack_v.shape[0] // n_dom
    slots = pack_v.shape[0]
    steps = n_edge // 2
    per = groups // CHUNKS
    edge_half = rows // 2
    sub = edge_half // CHUNKS
    right = lax.rem(me_z + 1, n_edge)
    left = lax.rem(me_z + n_edge - 1, n_edge)

    def load(i, src, dst):
        return pltpu.make_async_copy(src, dst, load_sem.at[i])

    edge_loads = [
        [
            load(2 * c + h, edges_h.at[pl.ds(h * edge_half + c * sub, sub)], edges_v.at[pl.ds(h * edge_half + c * sub, sub)])
            for h in range(2)
        ]
        for c in range(CHUNKS)
    ]
    base = 2 * CHUNKS
    we_load = load(base, we_h, we_v)
    others = [
        load(base + 1, tiles_h, tiles_v),
        load(base + 2, wup_h, wup_v),
        load(base + 3, wres_h, wres_v),
        load(base + 4, wmsg_h, wmsg_v),
        load(base + 5, watom_h, watom_v),
        load(base + 6, wjoin_h, wjoin_v),
    ]
    we_load.start()
    for pair in edge_loads:
        for one in pair:
            one.start()

    barrier = pltpu.get_barrier_semaphore()
    for peer in (left, right):
        pl.semaphore_signal(barrier, inc=1, device_id={"edge": peer}, device_id_type=MESH)

    def greet(k, carry):
        pl.semaphore_signal(
            barrier, inc=1, device_id={"dom": lax.rem(me_d + k, n_dom)}, device_id_type=MESH
        )
        return carry

    lax.fori_loop(1, n_dom, greet, 0)
    for one in others:
        one.start()

    def ring(direction, s, c, receiving):
        if direction == 0:
            slot = lax.rem(me_z - s - (1 if receiving else 0) + 2 * n_edge, n_edge)
            to = right
        else:
            slot = lax.rem(me_z + s + (1 if receiving else 0), n_edge)
            to = left
        view = gath.at[pl.ds(slot * groups + c * per, per)]
        return pltpu.make_async_remote_copy(
            src_ref=view,
            dst_ref=view,
            send_sem=ring_send.at[direction, s, c],
            recv_sem=ring_recv.at[direction, s, c],
            device_id={"edge": to},
            device_id_type=MESH,
        )

    zeros_down = jnp.zeros_like(wd_ref[...])
    wd_lo = jnp.concatenate([wd_ref[...], zeros_down], axis=0)
    wd_hi = jnp.concatenate([zeros_down, wd_ref[...]], axis=0)
    we_load.wait()
    for c in range(CHUNKS):
        for one in edge_loads[c]:
            one.wait()
        x = jnp.concatenate(
            [edges_v[pl.ds(c * sub, sub)], edges_v[pl.ds(edge_half + c * sub, sub)]], axis=0
        )
        hidden = silu(dot(x, we_v[...])).astype(BF16)
        narrow = silu(dot_nt(hidden[:sub], wd_lo) + dot_nt(hidden[sub:], wd_hi)).astype(BF16)
        gath[pl.ds(me_z * groups + c * per, per)] = narrow.reshape(per, narrow.shape[0] // per, narrow.shape[1])
        if c == 0:
            pl.semaphore_wait(barrier, n_dom + 1)
        ring(0, 0, c, False).start()
        ring(1, 0, c, False).start()

    shift = log2(rows * n_edge)
    rev_row = rev_ref[...]
    hold_row = lax.shift_right_logical(rev_row, shift)
    local_row = hold_row == me_d
    src_row = rev_row & (rows - 1)
    for i, row in enumerate((rev_row, ai_ref[0:1], ai_ref[1:2])):
        cols_v[i] = jnp.transpose(jnp.broadcast_to(row.astype(F32), (8, rows))).astype(I32)
    piece = rows // PIECES

    def forward(t):
        s, c = 1 + lax.div(t, CHUNKS), lax.rem(t, CHUNKS)
        for direction in range(2):
            ring(direction, s - 1, c, True).wait_recv()
            ring(direction, s, c, False).start()

    def ranks(i):
        at = i * piece
        here = pl.ds(at, piece)
        rev_col = cols_v[0, here, 0:1]
        hold_col = lax.shift_right_logical(rev_col, shift)
        before = (hold_col == hold_row) & (iota((piece, rows), 0) + at < iota((piece, rows), 1))
        rank_v[...] = rank_v[...] + jnp.sum(flag(before), axis=0, keepdims=True)
        lower = (rev_row >= lax.shift_left(hold_col, shift)) & (rev_row < rev_col)
        rank = jnp.sum(flag(lower), axis=1, keepdims=True).astype(I32)
        high = jnp.where(rank >= half_cap, 1, 0)
        code = jnp.where(hold_col == me_d, -1, hold_col * half_cap + rank - high * half_cap)
        rec_v[here] = flag(iota((piece, slots), 1) == code).astype(BF16)
        keep_v[here] = flag((iota((piece, 128), 1) >= 64) == (high == 1))

    def select(i):
        at = i * piece
        here = pl.ds(at, piece)
        rank = rank_v[0:1].astype(I32)
        high = jnp.where(rank >= half_cap, 1, 0)
        code = jnp.where(local_row, -1, hold_row * half_cap + rank + high * (slots - half_cap))
        at_slot = i * (2 * slots // PIECES)
        sel_v[pl.ds(at_slot, 2 * slots // PIECES)] = flag(
            iota((2 * slots // PIECES, rows), 0) + at_slot == code
        ).astype(BF16)
        rev_col = cols_v[0, here, 0:1]
        from_col = jnp.where(
            lax.shift_right_logical(rev_col, shift) == me_d, rev_col & (rows - 1), -1
        )
        loc_v[here] = flag(iota((piece, rows), 1) == from_col).astype(BF16)

    def onehots(i):
        here = pl.ds(i * piece, piece)
        atom_piece = part_atoms // PIECES
        tgt_t[pl.ds(i * atom_piece, atom_piece)] = flag(
            iota((atom_piece, rows), 0) + i * atom_piece == ai_ref[1:2]
        ).astype(BF16)
        lanes = iota((piece, part_atoms), 1)
        src_g[here] = flag(lanes == cols_v[1, here, 0:1]).astype(BF16)
        tgt_g[here] = flag(lanes == cols_v[2, here, 0:1]).astype(BF16)

    rank_v[...] = jnp.zeros_like(rank_v)
    middle = (steps - 2) * CHUNKS
    for k, work in enumerate((ranks, select, onehots)):

        def turn(i, carry, k=k, work=work):
            if k * PIECES < middle:
                forward(k * PIECES + i)
            work(i)
            return carry

        lax.fori_loop(0, PIECES, turn, 0)

    arr_v[pl.ds(me_d * half_cap, half_cap)] = jnp.zeros((half_cap, 128), BF16)

    last = steps - 1
    split = CHUNKS // 2
    for c in range(CHUNKS):
        for direction in range(2):
            ring(direction, last - 1, c, True).wait_recv()
            if (c < split) == (direction == 0):
                ring(direction, last, c, False).start()
    for c in range(CHUNKS):
        ring(0 if c < split else 1, last, c, True).wait_recv()

    others[0].wait()
    blocks = tiles_v.shape[0]
    lane_half = lax.shift_right_logical(iota((64, 128), 1), 6)
    for b in range(blocks):
        picked = []
        for k in range(2):
            source = ts_ref[k, b]
            owner = lax.shift_right_logical(source, log2(blocks))
            inner = source & (blocks - 1)
            value = gath[owner * groups + (inner & (groups - 1))]
            picked.append(
                jnp.where(lane_half == lax.shift_right_logical(inner, log2(groups)), value, jnp.zeros_like(value))
            )
        mixed = dot(tiles_v[b], jnp.concatenate(picked, axis=0))
        trip_v[pl.ds(b * 64, 64)] = (mixed + pltpu.roll(mixed, 64, 1)).astype(BF16)

    low_lanes = iota((slots, 128), 1) < 64
    pack_v[...] = jnp.where(
        low_lanes, dot(sel_v[pl.ds(0, slots)], trip_v[...]), dot(sel_v[pl.ds(slots, slots)], trip_v[...])
    ).astype(BF16)

    def send_dom(k, carry):
        peer = lax.rem(me_d + k, n_dom)
        pltpu.make_async_remote_copy(
            src_ref=pack_v.at[pl.ds(peer * half_cap, half_cap)],
            dst_ref=arr_v.at[pl.ds(me_d * half_cap, half_cap)],
            send_sem=x_sem.at[0],
            recv_sem=x_sem.at[1],
            device_id={"dom": peer},
            device_id_type=MESH,
        ).start()
        return carry

    lax.fori_loop(1, n_dom, send_dom, 0)
    all_but_one = pl.ds(0, slots - half_cap)
    exchange = pltpu.make_async_remote_copy(
        src_ref=pack_v.at[all_but_one],
        dst_ref=arr_v.at[all_but_one],
        send_sem=x_sem.at[0],
        recv_sem=x_sem.at[1],
        device_id={"dom": lax.rem(me_d + 1, n_dom)},
        device_id_type=MESH,
    )
    part = rows // 4
    for i in range(4):
        mir_v[pl.ds(i * part, part)] = dot(loc_v[pl.ds(i * part, part)], trip_v[...])
    for one in others[1:]:
        one.wait()
    exchange.wait()

    def edge_part(i, carry):
        here = pl.ds(i * part, part)
        found = dot(rec_v[here], arr_v[...]) * keep_v[here]
        mirrored = (found + pltpu.roll(found, 64, 1) + mir_v[here]).astype(BF16)
        both = jnp.where(iota((part, 128), 1) < 64, trip_v[here], mirrored)
        state = (edges_v[here].astype(F32) + dot(both, wup_v[...]) * ROOT_HALF).astype(BF16)
        middle = silu(dot(state, wres_v[0])).astype(BF16)
        branch = silu(dot(middle, wres_v[1]))
        state = ((state.astype(F32) + branch) * ROOT_HALF).astype(BF16)
        es_v[here] = state
        msg_v[here] = dot(state, wmsg_v[...]).astype(BF16)
        return carry

    for i in range(4):
        edge_part(i, 0)

    a_part = part_atoms // 4
    for i in range(4):
        here = pl.ds(i * a_part, a_part)
        rs_v[here] = dot(tgt_t[here], msg_v[...]).astype(BF16)

    def push(src, dst, sems, peer):
        pltpu.make_async_remote_copy(
            src_ref=src,
            dst_ref=dst,
            send_sem=z_sem.at[sems[0]],
            recv_sem=z_sem.at[sems[1]],
            device_id={"edge": peer},
            device_id_type=MESH,
        ).start()

    def local(ref, sems):
        return pltpu.make_async_remote_copy(
            src_ref=ref,
            dst_ref=ref,
            send_sem=z_sem.at[sems[0]],
            recv_sem=z_sem.at[sems[1]],
            device_id={"edge": right},
            device_id_type=MESH,
        )

    def away(d):
        return lax.rem(me_z + d + n_edge, n_edge)

    def atoms_of(device):
        return pl.ds(device * own_atoms, own_atoms)

    def slot_of(i):
        return pl.ds(i * own_atoms, own_atoms)

    hop = n_edge // 4
    for d in range(2 * hop, hop, -1):
        push(rs_v.at[atoms_of(away(d))], rel_v.at[slot_of(d - hop - 1)], (0, 1), away(d - hop))
        if d < 2 * hop:
            push(rs_v.at[atoms_of(away(-d))], rel_v.at[slot_of(d - 1)], (0, 1), away(hop - d))
    for d in range(hop - 1, 0, -1):
        push(rs_v.at[atoms_of(away(d))], fin_v.at[slot_of(d - 1)], (0, 2), away(d))
        push(rs_v.at[atoms_of(away(-d))], fin_v.at[slot_of(hop + d - 1)], (0, 2), away(-d))

    def pre_part(i, carry):
        here = pl.ds(i * part, part)
        pre_v[here] = dot(es_v[here], wjoin_v[pl.ds(2 * atom_width, width)])
        return carry

    local(rel_v, (0, 1)).wait_recv()
    for side, first, count in ((0, 0, hop), (1, hop, hop - 1)):
        owner = away(hop if side == 0 else -hop)
        relayed = rs_v[atoms_of(owner)].astype(F32)
        for i in range(first, first + count):
            relayed = relayed + rel_v[slot_of(i)].astype(F32)
        hop_v[slot_of(side)] = relayed.astype(BF16)
        push(hop_v.at[slot_of(side)], fin_v.at[slot_of((side + 1) * hop - 1)], (0, 2), owner)
    lax.fori_loop(0, 4, pre_part, 0)
    local(fin_v, (0, 2)).wait_recv()
    own = atoms_of(me_z)
    total = rs_v[own].astype(F32)
    for i in range(2 * hop):
        total = total + fin_v[slot_of(i)].astype(F32)
    scaled = (total * EPA ** (-0.5)).astype(BF16)
    middle_atoms = silu(dot(scaled, watom_v[0])).astype(BF16)
    fresh = (atoms_ref[...].astype(F32) + dot(middle_atoms, watom_v[1])).astype(BF16)
    natoms_ref[...] = fresh
    na_v[own] = fresh

    for d in range(hop, 0, -1):
        push(na_v.at[own], na_v.at[own], (3, 4 if d == hop else 6), away(d))
        push(na_v.at[own], na_v.at[own], (3, 5 if d == hop else 6), away(-d))
    for side in range(2):
        sign = 1 - 2 * side
        passed = na_v.at[atoms_of(away(-sign * hop))]
        local(passed, (3, 4 + side)).wait_recv()
        for d in range(hop - side, 0, -1):
            push(passed, passed, (3, 6), away(sign * d))
    local(na_v.at[pl.ds(0, (n_edge - 3) * own_atoms)], (3, 6)).wait_recv()

    def final_part(i, carry):
        here = pl.ds(i * part, part)
        ends = jnp.concatenate([dot(src_g[here], na_v[...]), dot(tgt_g[here], na_v[...])], axis=1).astype(BF16)
        update = silu(dot(ends, wjoin_v[pl.ds(0, 2 * atom_width)]) + pre_v[here])
        out_ref[here] = ((es_v[here].astype(F32) + update) * ROOT_HALF).astype(BF16)
        return carry

    for i in range(4):
        final_part(i, 0)

    most = pl.ds(0, part_atoms - own_atoms)
    local(rs_v.at[most], (0, 1)).wait_send()
    local(na_v.at[most], (3, 4)).wait_send()
    def drain(t, carry):
        s, c = lax.div(t, CHUNKS), lax.rem(t, CHUNKS)
        for direction in range(2):
            ring(direction, s, c, False).wait_send()
        return carry

    lax.fori_loop(0, last * CHUNKS, drain, 0)
    for c in range(CHUNKS):
        ring(0 if c < split else 1, last, c, False).wait_send()


def body(n_dom, n_edge, edges, atoms, reverse, atom_index, tile_source, tiles, weight_edge, weight_down, weight_up,
         weight_residual, weight_message, weight_atom, weight_join):
    rows, width = edges.shape
    own_atoms, atom_width = atoms.shape
    part_atoms = own_atoms * n_edge
    blocks = tiles.shape[0]
    channels = weight_down.shape[0]
    assert channels == 64 and tiles.shape[1:] == (64, 128)
    groups = blocks // 2
    capacity = rows // n_dom
    slots = n_dom * capacity // 2
    vmem = pl.BlockSpec(memory_space=pltpu.VMEM)
    hbm = pl.BlockSpec(memory_space=pl.ANY)
    return pl.pallas_call(
        functools.partial(kernel, n_dom, n_edge),
        out_shape=(
            jax.ShapeDtypeStruct((rows, width), BF16),
            jax.ShapeDtypeStruct((own_atoms, atom_width), BF16),
        ),
        in_specs=[pl.BlockSpec(memory_space=pltpu.SMEM)] + [vmem] * 4 + [hbm] * 8,
        out_specs=(vmem, vmem),
        scratch_shapes=[
            pltpu.VMEM((rows, width), BF16),
            pltpu.VMEM(tiles.shape, BF16),
            pltpu.VMEM(weight_edge.shape, BF16),
            pltpu.VMEM((2 * channels, width), BF16),
            pltpu.VMEM((2, width, width), BF16),
            pltpu.VMEM(weight_message.shape, BF16),
            pltpu.VMEM(weight_atom.shape, BF16),
            pltpu.VMEM(weight_join.shape, BF16),
            pltpu.VMEM((n_edge * groups, 64, 128), BF16),
            pltpu.VMEM((rows, 128), BF16),
            pltpu.VMEM((slots, 128), BF16),
            pltpu.VMEM((slots, 128), BF16),
            pltpu.VMEM((rows, 128), F32),
            pltpu.VMEM((2 * slots, rows), BF16),
            pltpu.VMEM((rows, rows), BF16),
            pltpu.VMEM((rows, slots), BF16),
            pltpu.VMEM((rows, 128), F32),
            pltpu.VMEM((part_atoms, rows), BF16),
            pltpu.VMEM((rows, part_atoms), BF16),
            pltpu.VMEM((rows, part_atoms), BF16),
            pltpu.VMEM((3, rows, 8), I32),
            pltpu.VMEM((8, rows), F32),
            pltpu.VMEM((rows, width), BF16),
            pltpu.VMEM((rows, atom_width), BF16),
            pltpu.VMEM((rows, width), F32),
            pltpu.VMEM((part_atoms, atom_width), BF16),
            pltpu.VMEM((part_atoms // 2 - own_atoms, atom_width), BF16),
            pltpu.VMEM((2 * own_atoms, atom_width), BF16),
            pltpu.VMEM((part_atoms // 2, atom_width), BF16),
            pltpu.VMEM((part_atoms, atom_width), BF16),
            pltpu.SemaphoreType.DMA((2 * CHUNKS + 7,)),
            pltpu.SemaphoreType.DMA((2, n_edge // 2, CHUNKS)),
            pltpu.SemaphoreType.DMA((2, n_edge // 2, CHUNKS)),
            pltpu.SemaphoreType.DMA((2,)),
            pltpu.SemaphoreType.DMA((7,)),
        ],
        compiler_params=pltpu.CompilerParams(
            collective_id=0, has_side_effects=True, vmem_limit_bytes=56 * 1024 * 1024
        ),
    )(
        tile_source.T,
        reverse.reshape(1, rows),
        atom_index,
        atoms,
        weight_down,
        edges,
        tiles,
        weight_edge,
        weight_up.reshape(2 * channels, width),
        weight_residual.reshape(2, width, width),
        weight_message,
        weight_atom,
        weight_join,
    )


def solution(mesh):
    n_dom, n_edge = mesh.shape["dom"], mesh.shape["edge"]
    placed = (
        P(("dom", "edge"), None),
        P(("dom", "edge"), None),
        P(("dom", "edge")),
        P(None, ("dom", "edge")),
        P(("dom", "edge"), None),
        P(("dom", "edge"), None, None),
        P(),
        P(),
        P(),
        P(),
        P(),
        P(),
        P(),
    )
    return jax.shard_map(
        functools.partial(body, n_dom, n_edge),
        mesh=mesh,
        in_specs=placed,
        out_specs=(P(("dom", "edge"), None), P(("dom", "edge"), None)),
        check_vma=False,
    )
```

```python
import functools

import jax
import jax.numpy as jnp
from jax import lax
from jax.experimental import pallas as pl
from jax.experimental.pallas import tpu as pltpu
from jax.sharding import PartitionSpec as P

EPA = 32
ROOT_HALF = 0.7071067811865476
MESH = pl.DeviceIdType.MESH
BF16 = jnp.bfloat16
F32 = jnp.float32
I32 = jnp.int32
CHUNKS = 4
PIECES = 16


def silu(v):
    half = 0.5 * v
    return half + half * jnp.tanh(half)


def dot(a, b):
    return jnp.dot(a, b, preferred_element_type=F32)


def dot_nt(a, b):
    return lax.dot_general(a, b, (((1,), (1,)), ((), ())), preferred_element_type=F32)


def iota(shape, axis):
    return lax.broadcasted_iota(I32, shape, axis)


def log2(n):
    assert n & (n - 1) == 0
    return n.bit_length() - 1


def flag(cond):
    return jnp.where(cond, jnp.float32(1), jnp.float32(0))


def kernel(
    n_dom,
    n_edge,
    ts_h,
    rev_h,
    ai_h,
    atoms_h,
    wd_h,
    edges_h,
    tiles_h,
    we_h,
    wup_h,
    wres_h,
    wmsg_h,
    watom_h,
    wjoin_h,
    natoms_ref,
    es_v,
    pre_v,
    na_v,
    src_g,
    tgt_g,
    wjoin_v,
    edges_v,
    tiles_v,
    we_v,
    wup_v,
    wres_v,
    wmsg_v,
    watom_v,
    ts_ref,
    rev_ref,
    ai_ref,
    atoms_ref,
    wd_ref,
    gath,
    trip_v,
    pack_v,
    arr_v,
    mir_v,
    sel_v,
    loc_v,
    rec_v,
    keep_v,
    tgt_t,
    cols_v,
    rank_v,
    msg_v,
    rs_v,
    rel_v,
    hop_v,
    fin_v,
    load_sem,
    ring_send,
    ring_recv,
    x_sem,
    z_sem,
):
    me_d = lax.axis_index("dom")
    me_z = lax.axis_index("edge")
    rows, width = edges_v.shape
    groups = gath.shape[0] // n_edge
    part_atoms, atom_width = rs_v.shape
    own_atoms = part_atoms // n_edge
    half_cap = pack_v.shape[0] // n_dom
    slots = pack_v.shape[0]
    steps = n_edge // 2
    per = groups // CHUNKS
    edge_half = rows // 2
    sub = edge_half // CHUNKS
    right = lax.rem(me_z + 1, n_edge)
    left = lax.rem(me_z + n_edge - 1, n_edge)

    def load(i, src, dst):
        return pltpu.make_async_copy(src, dst, load_sem.at[i])

    edge_loads = [
        [
            load(2 * c + h, edges_h.at[pl.ds(h * edge_half + c * sub, sub)], edges_v.at[pl.ds(h * edge_half + c * sub, sub)])
            for h in range(2)
        ]
        for c in range(CHUNKS)
    ]
    base = 2 * CHUNKS
    we_load = load(base, we_h, we_v)
    others = [
        load(base + 1, tiles_h, tiles_v),
        load(base + 2, wup_h, wup_v),
        load(base + 3, wres_h, wres_v),
        load(base + 4, wmsg_h, wmsg_v),
        load(base + 5, watom_h, watom_v),
        load(base + 6, wjoin_h, wjoin_v),
    ]
    wd_load = load(base + 7, wd_h, wd_ref)
    index_loads = [load(base + 8, rev_h, rev_ref), load(base + 9, ai_h, ai_ref), load(base + 10, atoms_h, atoms_ref),
                   load(base + 11, ts_h, ts_ref)]
    we_load.start()
    for c in (c for j in range(CHUNKS // 2) for c in (j, j + CHUNKS // 2)):
        for one in edge_loads[c]:
            one.start()

    wd_load.start()
    for one in index_loads:
        one.start()

    barrier = pltpu.get_barrier_semaphore()
    for peer in (left, right):
        pl.semaphore_signal(barrier, inc=1, device_id={"edge": peer}, device_id_type=MESH)

    def greet(k, carry):
        pl.semaphore_signal(
            barrier, inc=1, device_id={"dom": lax.rem(me_d + k, n_dom)}, device_id_type=MESH
        )
        return carry

    lax.fori_loop(1, n_dom, greet, 0)
    for one in others:
        one.start()

    def ring(direction, s, c, receiving):
        if direction == 0:
            slot = lax.rem(me_z - s - (1 if receiving else 0) + 2 * n_edge, n_edge)
            to = right
        else:
            slot = lax.rem(me_z + s + (1 if receiving else 0), n_edge)
            to = left
        view = gath.at[pl.ds(slot * groups + c * per, per)]
        return pltpu.make_async_remote_copy(
            src_ref=view,
            dst_ref=view,
            send_sem=ring_send.at[direction, s, c],
            recv_sem=ring_recv.at[direction, s, c],
            device_id={"edge": to},
            device_id_type=MESH,
        )

    wd_load.wait()
    zeros_down = jnp.zeros_like(wd_ref[...])
    wd_lo = jnp.concatenate([wd_ref[...], zeros_down], axis=0)
    wd_hi = jnp.concatenate([zeros_down, wd_ref[...]], axis=0)
    orders = [[c for c in range(CHUNKS)], [(c + CHUNKS // 2) % CHUNKS for c in range(CHUNKS)]]
    we_load.wait()
    for j in range(CHUNKS):
        c = orders[j % 2][j // 2]
        for one in edge_loads[c]:
            one.wait()
        x = jnp.concatenate(
            [edges_v[pl.ds(c * sub, sub)], edges_v[pl.ds(edge_half + c * sub, sub)]], axis=0
        )
        hidden = silu(dot(x, we_v[...])).astype(BF16)
        narrow = silu(dot_nt(hidden[:sub], wd_lo) + dot_nt(hidden[sub:], wd_hi)).astype(BF16)
        gath[pl.ds(me_z * groups + c * per, per)] = narrow.reshape(per, narrow.shape[0] // per, narrow.shape[1])
        if j == 0:
            pl.semaphore_wait(barrier, n_dom + 1)
        ring(j % 2, 0, c, False).start()
    for j in range(CHUNKS // 2, CHUNKS):
        for direction in range(2):
            ring(direction, 0, orders[direction][j], False).start()

    shift = log2(rows * n_edge)
    for one in index_loads:
        one.wait()
    rev_row = rev_ref[...]
    hold_row = lax.shift_right_logical(rev_row, shift)
    local_row = hold_row == me_d
    src_row = rev_row & (rows - 1)
    for i, row in enumerate((rev_row, ai_ref[0:1], ai_ref[1:2])):
        cols_v[i] = jnp.transpose(jnp.broadcast_to(row.astype(F32), (8, rows))).astype(I32)
    piece = rows // PIECES

    def forward(t):
        s, at = 1 + lax.div(t, CHUNKS), lax.rem(t, CHUNKS)
        for direction in range(2):
            c = at if direction == 0 else lax.rem(at + CHUNKS // 2, CHUNKS)
            ring(direction, s - 1, c, True).wait_recv()
            ring(direction, s, c, False).start()

    def ranks(i):
        at = i * piece
        here = pl.ds(at, piece)
        rev_col = cols_v[0, here, 0:1]
        hold_col = lax.shift_right_logical(rev_col, shift)
        before = (hold_col == hold_row) & (iota((piece, rows), 0) + at < iota((piece, rows), 1))
        rank_v[...] = rank_v[...] + jnp.sum(flag(before), axis=0, keepdims=True)
        lower = (rev_row >= lax.shift_left(hold_col, shift)) & (rev_row < rev_col)
        rank = jnp.sum(flag(lower), axis=1, keepdims=True).astype(I32)
        cols_v[3, here] = jnp.broadcast_to(rank, (piece, 8))

    def select(i):
        at = i * piece
        here = pl.ds(at, piece)
        rank = rank_v[0:1].astype(I32)
        high = jnp.where(rank >= half_cap, 1, 0)
        code = jnp.where(local_row, -1, hold_row * half_cap + rank + high * (slots - half_cap))
        at_slot = i * (2 * slots // PIECES)
        sel_v[pl.ds(at_slot, 2 * slots // PIECES)] = flag(
            iota((2 * slots // PIECES, rows), 0) + at_slot == code
        ).astype(BF16)
        rev_col = cols_v[0, here, 0:1]
        from_col = jnp.where(
            lax.shift_right_logical(rev_col, shift) == me_d, rev_col & (rows - 1), -1
        )
        loc_v[here] = flag(iota((piece, rows), 1) == from_col).astype(BF16)

    def receive(i, carry):
        here = pl.ds(i * piece, piece)
        hold_col = lax.shift_right_logical(cols_v[0, here, 0:1], shift)
        rank = cols_v[3, here, 0:1]
        high = jnp.where(rank >= half_cap, 1, 0)
        code = jnp.where(hold_col == me_d, -1, hold_col * half_cap + rank - high * half_cap)
        rec_v[here] = flag(iota((piece, slots), 1) == code).astype(BF16)
        keep_v[here] = flag((iota((piece, 128), 1) >= 64) == (high == 1))
        atom_piece = part_atoms // PIECES
        tgt_t[pl.ds(i * atom_piece, atom_piece)] = flag(
            iota((atom_piece, rows), 0) + i * atom_piece == ai_ref[1:2]
        ).astype(BF16)
        return carry

    def ends(i, carry):
        here = pl.ds(i * piece, piece)
        lanes = iota((piece, part_atoms), 1)
        src_g[here] = flag(lanes == cols_v[1, here, 0:1]).astype(BF16)
        tgt_g[here] = flag(lanes == cols_v[2, here, 0:1]).astype(BF16)
        return carry

    rank_v[...] = jnp.zeros_like(rank_v)
    middle = (steps - 2) * CHUNKS

    def first_turn(i, carry):
        if middle >= PIECES // 2:
            forward(i)
        ranks(2 * i)
        ranks(2 * i + 1)
        return carry

    def second_turn(i, carry):
        if middle >= 3 * PIECES // 2:
            forward(PIECES // 2 + i)
        select(i)
        return carry

    assert middle in (0, PIECES // 2, 3 * PIECES // 2)
    lax.fori_loop(0, PIECES // 2, first_turn, 0)
    lax.fori_loop(0, PIECES, second_turn, 0)

    arr_v[pl.ds(me_d * half_cap, half_cap)] = jnp.zeros((half_cap, 128), BF16)

    last = steps - 1
    split = CHUNKS // 2
    for j in range(CHUNKS):
        for direction in range(2):
            c = orders[direction][j]
            ring(direction, last - 1, c, True).wait_recv()
            if j < split:
                ring(direction, last, c, False).start()
    for j in range(split):
        for direction in range(2):
            ring(direction, last, orders[direction][j], True).wait_recv()

    others[0].wait()
    blocks = tiles_v.shape[0]
    lane_half = lax.shift_right_logical(iota((64, 128), 1), 6)
    for b in range(blocks):
        picked = []
        for k in range(2):
            source = ts_ref[k, b]
            owner = lax.shift_right_logical(source, log2(blocks))
            inner = source & (blocks - 1)
            value = gath[owner * groups + (inner & (groups - 1))]
            picked.append(
                jnp.where(lane_half == lax.shift_right_logical(inner, log2(groups)), value, jnp.zeros_like(value))
            )
        mixed = dot(tiles_v[b], jnp.concatenate(picked, axis=0))
        trip_v[pl.ds(b * 64, 64)] = (mixed + pltpu.roll(mixed, 64, 1)).astype(BF16)

    low_lanes = iota((slots, 128), 1) < 64
    pack_v[...] = jnp.where(
        low_lanes, dot(sel_v[pl.ds(0, slots)], trip_v[...]), dot(sel_v[pl.ds(slots, slots)], trip_v[...])
    ).astype(BF16)

    def send_dom(k, carry):
        peer = lax.rem(me_d + k, n_dom)
        pltpu.make_async_remote_copy(
            src_ref=pack_v.at[pl.ds(peer * half_cap, half_cap)],
            dst_ref=arr_v.at[pl.ds(me_d * half_cap, half_cap)],
            send_sem=x_sem.at[0],
            recv_sem=x_sem.at[1],
            device_id={"dom": peer},
            device_id_type=MESH,
        ).start()
        return carry

    lax.fori_loop(1, n_dom, send_dom, 0)
    all_but_one = pl.ds(0, slots - half_cap)
    exchange = pltpu.make_async_remote_copy(
        src_ref=pack_v.at[all_but_one],
        dst_ref=arr_v.at[all_but_one],
        send_sem=x_sem.at[0],
        recv_sem=x_sem.at[1],
        device_id={"dom": lax.rem(me_d + 1, n_dom)},
        device_id_type=MESH,
    )
    lax.fori_loop(0, PIECES, receive, 0)
    part = rows // 4
    for i in range(4):
        mir_v[pl.ds(i * part, part)] = dot(loc_v[pl.ds(i * part, part)], trip_v[...])
    for one in others[1:]:
        one.wait()
    exchange.wait()

    def edge_part(i, carry):
        here = pl.ds(i * part, part)
        found = dot(rec_v[here], arr_v[...]) * keep_v[here]
        mirrored = (found + pltpu.roll(found, 64, 1) + mir_v[here]).astype(BF16)
        both = jnp.where(iota((part, 128), 1) < 64, trip_v[here], mirrored)
        state = (edges_v[here].astype(F32) + dot(both, wup_v[...]) * ROOT_HALF).astype(BF16)
        middle = silu(dot(state, wres_v[0])).astype(BF16)
        branch = silu(dot(middle, wres_v[1]))
        state = ((state.astype(F32) + branch) * ROOT_HALF).astype(BF16)
        es_v[here] = state
        msg_v[here] = dot(state, wmsg_v[...]).astype(BF16)
        return carry

    for i in range(4):
        edge_part(i, 0)

    a_part = part_atoms // 4
    for i in range(4):
        here = pl.ds(i * a_part, a_part)
        rs_v[here] = dot(tgt_t[here], msg_v[...]).astype(BF16)

    def push(src, dst, sems, peer):
        pltpu.make_async_remote_copy(
            src_ref=src,
            dst_ref=dst,
            send_sem=z_sem.at[sems[0]],
            recv_sem=z_sem.at[sems[1]],
            device_id={"edge": peer},
            device_id_type=MESH,
        ).start()

    def local(ref, sems):
        return pltpu.make_async_remote_copy(
            src_ref=ref,
            dst_ref=ref,
            send_sem=z_sem.at[sems[0]],
            recv_sem=z_sem.at[sems[1]],
            device_id={"edge": right},
            device_id_type=MESH,
        )

    def away(d):
        return lax.rem(me_z + d + n_edge, n_edge)

    def atoms_of(device):
        return pl.ds(device * own_atoms, own_atoms)

    def slot_of(i):
        return pl.ds(i * own_atoms, own_atoms)

    hop = n_edge // 4
    half_own = own_atoms // 2

    def half_of(device, side):
        return pl.ds(device * own_atoms + side * half_own, half_own)

    for side in range(2):
        sign = 1 - 2 * side
        push(
            rs_v.at[half_of(away(sign * 2 * hop), side)],
            rel_v.at[half_of(side * hop + hop - 1, side)],
            (0, 1),
            away(sign * hop),
        )
    for d in range(2 * hop - 1, hop, -1):
        for side in range(2):
            sign = 1 - 2 * side
            push(
                rs_v.at[atoms_of(away(sign * d))],
                rel_v.at[slot_of(side * hop + d - hop - 1)],
                (0, 1),
                away(sign * (d - hop)),
            )
    for d in range(hop - 1, 0, -1):
        push(rs_v.at[atoms_of(away(d))], fin_v.at[slot_of(d - 1)], (0, 2), away(d))
        push(rs_v.at[atoms_of(away(-d))], fin_v.at[slot_of(hop + d - 1)], (0, 2), away(-d))
    for side in range(2):
        rel_v[half_of(side * hop + hop - 1, 1 - side)] = jnp.zeros((half_own, atom_width), BF16)
    lax.fori_loop(0, PIECES, ends, 0)

    def pre_part(i, carry):
        here = pl.ds(i * part, part)
        pre_v[here] = dot(es_v[here], wjoin_v[pl.ds(2 * atom_width, width)])
        return carry

    local(rel_v.at[pl.ds(0, (2 * hop - 1) * own_atoms)], (0, 1)).wait_recv()
    for side in range(2):
        owner = away(hop if side == 0 else -hop)
        relayed = rs_v[atoms_of(owner)].astype(F32)
        for i in range(hop):
            relayed = relayed + rel_v[slot_of(side * hop + i)].astype(F32)
        hop_v[slot_of(side)] = relayed.astype(BF16)
        push(hop_v.at[slot_of(side)], fin_v.at[slot_of((side + 1) * hop - 1)], (0, 2), owner)
    lax.fori_loop(0, 4, pre_part, 0)
    local(fin_v, (0, 2)).wait_recv()
    own = atoms_of(me_z)
    total = rs_v[own].astype(F32)
    for i in range(2 * hop):
        total = total + fin_v[slot_of(i)].astype(F32)
    scaled = (total * EPA ** (-0.5)).astype(BF16)
    middle_atoms = silu(dot(scaled, watom_v[0])).astype(BF16)
    fresh = (atoms_ref[...].astype(F32) + dot(middle_atoms, watom_v[1])).astype(BF16)
    natoms_ref[...] = fresh
    na_v[own] = fresh

    for d in range(hop, 0, -1):
        push(na_v.at[own], na_v.at[own], (3, 4 if d == hop else 6), away(d))
        push(na_v.at[own], na_v.at[own], (3, 5 if d == hop else 6), away(-d))
    for side in range(2):
        sign = 1 - 2 * side
        passed = na_v.at[atoms_of(away(-sign * hop))]
        local(passed, (3, 4 + side)).wait_recv()
        far = na_v.at[half_of(away(-sign * hop), side)]
        push(far, far, (3, 6), away(sign * hop))
        for d in range(hop - 1, 0, -1):
            push(passed, passed, (3, 6), away(sign * d))
    local(na_v.at[pl.ds(0, (n_edge - 3) * own_atoms)], (3, 6)).wait_recv()

    most = pl.ds(0, part_atoms - own_atoms)
    local(rs_v.at[most], (0, 1)).wait_send()
    local(na_v.at[most], (3, 4)).wait_send()
    def drain(t, carry):
        s, c = lax.div(t, CHUNKS), lax.rem(t, CHUNKS)
        for direction in range(2):
            ring(direction, s, c, False).wait_send()
        return carry

    lax.fori_loop(0, last * CHUNKS, drain, 0)
    for j in range(split):
        for direction in range(2):
            ring(direction, last, orders[direction][j], False).wait_send()


def finish(fresh_ref, es_ref, pre_ref, na_ref, src_ref, tgt_ref, wjoin_ref, out_h, natoms_ref, out_v, sem):
    rows = es_ref.shape[0]
    part = rows // 4
    natoms_ref[...] = fresh_ref[...]
    copies = []
    for i in range(4):
        here = pl.ds(i * part, part)
        ends = jnp.concatenate([dot(src_ref[here], na_ref[...]), dot(tgt_ref[here], na_ref[...])], axis=1).astype(BF16)
        update = silu(dot(ends, wjoin_ref[pl.ds(0, 2 * na_ref.shape[1])]) + pre_ref[here])
        out_v[here] = ((es_ref[here].astype(F32) + update) * ROOT_HALF).astype(BF16)
        copies.append(pltpu.make_async_copy(out_v.at[here], out_h.at[here], sem.at[i]))
        copies[-1].start()
    for one in copies:
        one.wait()


def body(n_dom, n_edge, edges, atoms, reverse, atom_index, tile_source, tiles, weight_edge, weight_down, weight_up,
         weight_residual, weight_message, weight_atom, weight_join):
    rows, width = edges.shape
    own_atoms, atom_width = atoms.shape
    part_atoms = own_atoms * n_edge
    blocks = tiles.shape[0]
    channels = weight_down.shape[0]
    assert channels == 64 and tiles.shape[1:] == (64, 128)
    groups = blocks // 2
    capacity = rows // n_dom
    slots = n_dom * capacity // 2
    vmem = pl.BlockSpec(memory_space=pltpu.VMEM)
    hbm = pl.BlockSpec(memory_space=pltpu.HBM)
    fresh, state, pre, everyone, src_hot, tgt_hot, join = pl.pallas_call(
        functools.partial(kernel, n_dom, n_edge),
        out_shape=(
            jax.ShapeDtypeStruct((own_atoms, atom_width), BF16),
            jax.ShapeDtypeStruct((rows, width), BF16),
            jax.ShapeDtypeStruct((rows, width), F32),
            jax.ShapeDtypeStruct((part_atoms, atom_width), BF16),
            jax.ShapeDtypeStruct((rows, part_atoms), BF16),
            jax.ShapeDtypeStruct((rows, part_atoms), BF16),
            jax.ShapeDtypeStruct(weight_join.shape, BF16),
        ),
        in_specs=[hbm] * 13,
        out_specs=(vmem,) * 7,
        scratch_shapes=[
            pltpu.VMEM((rows, width), BF16),
            pltpu.VMEM(tiles.shape, BF16),
            pltpu.VMEM(weight_edge.shape, BF16),
            pltpu.VMEM((2 * channels, width), BF16),
            pltpu.VMEM((2, width, width), BF16),
            pltpu.VMEM(weight_message.shape, BF16),
            pltpu.VMEM(weight_atom.shape, BF16),
            pltpu.SMEM(tile_source.shape[::-1], I32),
            pltpu.VMEM((1, rows), I32),
            pltpu.VMEM((2, rows), I32),
            pltpu.VMEM((own_atoms, atom_width), BF16),
            pltpu.VMEM(weight_down.shape, BF16),
            pltpu.VMEM((n_edge * groups, 64, 128), BF16),
            pltpu.VMEM((rows, 128), BF16),
            pltpu.VMEM((slots, 128), BF16),
            pltpu.VMEM((slots, 128), BF16),
            pltpu.VMEM((rows, 128), F32),
            pltpu.VMEM((2 * slots, rows), BF16),
            pltpu.VMEM((rows, rows), BF16),
            pltpu.VMEM((rows, slots), BF16),
            pltpu.VMEM((rows, 128), F32),
            pltpu.VMEM((part_atoms, rows), BF16),
            pltpu.VMEM((4, rows, 8), I32),
            pltpu.VMEM((8, rows), F32),
            pltpu.VMEM((rows, atom_width), BF16),
            pltpu.VMEM((part_atoms, atom_width), BF16),
            pltpu.VMEM((part_atoms // 2, atom_width), BF16),
            pltpu.VMEM((2 * own_atoms, atom_width), BF16),
            pltpu.VMEM((part_atoms // 2, atom_width), BF16),
            pltpu.SemaphoreType.DMA((2 * CHUNKS + 12,)),
            pltpu.SemaphoreType.DMA((2, n_edge // 2, CHUNKS)),
            pltpu.SemaphoreType.DMA((2, n_edge // 2, CHUNKS)),
            pltpu.SemaphoreType.DMA((2,)),
            pltpu.SemaphoreType.DMA((7,)),
        ],
        compiler_params=pltpu.CompilerParams(
            collective_id=0, has_side_effects=True, vmem_limit_bytes=34 * 1024 * 1024
        ),
    )(
        *(
            pltpu.with_memory_space_constraint(one, pltpu.HBM)
            for one in (
                tile_source.T,
                reverse.reshape(1, rows),
                atom_index,
                atoms,
                weight_down,
                edges,
                tiles,
                weight_edge,
                weight_up.reshape(2 * channels, width),
                weight_residual.reshape(2, width, width),
                weight_message,
                weight_atom,
                weight_join,
            )
        ),
    )
    return pl.pallas_call(
        finish,
        out_shape=(
            jax.ShapeDtypeStruct((rows, width), BF16),
            jax.ShapeDtypeStruct((own_atoms, atom_width), BF16),
        ),
        in_specs=[vmem] * 7,
        out_specs=(hbm, vmem),
        scratch_shapes=[pltpu.VMEM((rows, width), BF16), pltpu.SemaphoreType.DMA((4,))],
        compiler_params=pltpu.CompilerParams(vmem_limit_bytes=12 * 1024 * 1024),
    )(fresh, state, pre, everyone, src_hot, tgt_hot, join)


def solution(mesh):
    n_dom, n_edge = mesh.shape["dom"], mesh.shape["edge"]
    placed = (
        P(("dom", "edge"), None),
        P(("dom", "edge"), None),
        P(("dom", "edge")),
        P(None, ("dom", "edge")),
        P(("dom", "edge"), None),
        P(("dom", "edge"), None, None),
        P(),
        P(),
        P(),
        P(),
        P(),
        P(),
        P(),
    )
    return jax.shard_map(
        functools.partial(body, n_dom, n_edge),
        mesh=mesh,
        in_specs=placed,
        out_specs=(P(("dom", "edge"), None), P(("dom", "edge"), None)),
        check_vma=False,
    )
```

```python
import functools

import jax
import jax.numpy as jnp
from jax import lax
from jax.experimental import pallas as pl
from jax.experimental.pallas import tpu as pltpu
from jax.sharding import PartitionSpec as P

EPA = 32
ROOT_HALF = 0.7071067811865476
MESH = pl.DeviceIdType.MESH
BF16 = jnp.bfloat16
F32 = jnp.float32
I32 = jnp.int32
CHUNKS = 4
PIECES = 16


def silu(v):
    half = 0.5 * v
    return half + half * jnp.tanh(half)


def dot(a, b):
    return jnp.dot(a, b, preferred_element_type=F32)


def dot_nt(a, b):
    return lax.dot_general(a, b, (((1,), (1,)), ((), ())), preferred_element_type=F32)


def iota(shape, axis):
    return lax.broadcasted_iota(I32, shape, axis)


def log2(n):
    assert n & (n - 1) == 0
    return n.bit_length() - 1


def flag(cond):
    return jnp.where(cond, jnp.float32(1), jnp.float32(0))


def kernel(
    n_dom,
    n_edge,
    ts_h,
    rev_h,
    ai_h,
    atoms_h,
    wd_h,
    edges_h,
    tiles_h,
    we_h,
    wup_h,
    wres_h,
    wmsg_h,
    watom_h,
    wjoin_h,
    natoms_ref,
    es_v,
    pre_v,
    na_v,
    src_g,
    tgt_g,
    wjoin_v,
    edges_v,
    tiles_v,
    we_v,
    wup_v,
    wres_v,
    wmsg_v,
    watom_v,
    ts_ref,
    rev_ref,
    ai_ref,
    atoms_ref,
    wd_ref,
    gath,
    trip_v,
    pack_v,
    arr_v,
    mir_v,
    sel_v,
    loc_v,
    rec_v,
    keep_v,
    tgt_t,
    cols_v,
    rank_v,
    msg_v,
    rs_v,
    rel_v,
    hop_v,
    fin_v,
    load_sem,
    ring_send,
    ring_recv,
    x_sem,
    z_sem,
):
    me_d = lax.axis_index("dom")
    me_z = lax.axis_index("edge")
    rows, width = edges_v.shape
    groups = gath.shape[0] // n_edge
    part_atoms, atom_width = rs_v.shape
    own_atoms = part_atoms // n_edge
    half_cap = pack_v.shape[0] // n_dom
    slots = pack_v.shape[0]
    steps = n_edge // 2
    per = groups // CHUNKS
    edge_half = rows // 2
    sub = edge_half // CHUNKS
    right = lax.rem(me_z + 1, n_edge)
    left = lax.rem(me_z + n_edge - 1, n_edge)

    def load(i, src, dst):
        return pltpu.make_async_copy(src, dst, load_sem.at[i])

    edge_loads = [
        [
            load(2 * c + h, edges_h.at[pl.ds(h * edge_half + c * sub, sub)], edges_v.at[pl.ds(h * edge_half + c * sub, sub)])
            for h in range(2)
        ]
        for c in range(CHUNKS)
    ]
    base = 2 * CHUNKS
    we_load = load(base, we_h, we_v)
    others = [
        load(base + 1, tiles_h, tiles_v),
        load(base + 2, wup_h, wup_v),
        load(base + 3, wres_h, wres_v),
        load(base + 4, wmsg_h, wmsg_v),
        load(base + 5, watom_h, watom_v),
        load(base + 6, wjoin_h, wjoin_v),
    ]
    wd_load = load(base + 7, wd_h, wd_ref)
    index_loads = [load(base + 8, rev_h, rev_ref), load(base + 9, ai_h, ai_ref), load(base + 10, atoms_h, atoms_ref),
                   load(base + 11, ts_h, ts_ref)]
    we_load.start()
    for c in (c for j in range(CHUNKS // 2) for c in (j, j + CHUNKS // 2)):
        for one in edge_loads[c]:
            one.start()

    wd_load.start()
    for one in index_loads:
        one.start()

    barrier = pltpu.get_barrier_semaphore()
    for peer in (left, right):
        pl.semaphore_signal(barrier, inc=1, device_id={"edge": peer}, device_id_type=MESH)

    def greet(k, carry):
        pl.semaphore_signal(
            barrier, inc=1, device_id={"dom": lax.rem(me_d + k, n_dom)}, device_id_type=MESH
        )
        return carry

    lax.fori_loop(1, n_dom, greet, 0)
    for one in others:
        one.start()

    def ring(direction, s, c, receiving):
        if direction == 0:
            slot = lax.rem(me_z - s - (1 if receiving else 0) + 2 * n_edge, n_edge)
            to = right
        else:
            slot = lax.rem(me_z + s + (1 if receiving else 0), n_edge)
            to = left
        view = gath.at[pl.ds(slot * groups + c * per, per)]
        return pltpu.make_async_remote_copy(
            src_ref=view,
            dst_ref=view,
            send_sem=ring_send.at[direction, s, c],
            recv_sem=ring_recv.at[direction, s, c],
            device_id={"edge": to},
            device_id_type=MESH,
        )

    wd_load.wait()
    zeros_down = jnp.zeros_like(wd_ref[...])
    wd_lo = jnp.concatenate([wd_ref[...], zeros_down], axis=0)
    wd_hi = jnp.concatenate([zeros_down, wd_ref[...]], axis=0)
    orders = [[c for c in range(CHUNKS)], [(c + CHUNKS // 2) % CHUNKS for c in range(CHUNKS)]]
    we_load.wait()
    for j in range(CHUNKS):
        c = orders[j % 2][j // 2]
        for one in edge_loads[c]:
            one.wait()
        x = jnp.concatenate(
            [edges_v[pl.ds(c * sub, sub)], edges_v[pl.ds(edge_half + c * sub, sub)]], axis=0
        )
        hidden = silu(dot(x, we_v[...])).astype(BF16)
        narrow = silu(dot_nt(hidden[:sub], wd_lo) + dot_nt(hidden[sub:], wd_hi)).astype(BF16)
        gath[pl.ds(me_z * groups + c * per, per)] = narrow.reshape(per, narrow.shape[0] // per, narrow.shape[1])
        if j == 0:
            pl.semaphore_wait(barrier, n_dom + 1)
        ring(j % 2, 0, c, False).start()
    for j in range(CHUNKS // 2, CHUNKS):
        for direction in range(2):
            ring(direction, 0, orders[direction][j], False).start()

    shift = log2(rows * n_edge)
    for one in index_loads:
        one.wait()
    rev_row = rev_ref[...]
    hold_row = lax.shift_right_logical(rev_row, shift)
    local_row = hold_row == me_d
    src_row = rev_row & (rows - 1)
    for i, row in enumerate((rev_row, ai_ref[0:1], ai_ref[1:2])):
        cols_v[i] = jnp.transpose(jnp.broadcast_to(row.astype(F32), (8, rows))).astype(I32)
    piece = rows // PIECES

    def forward(t):
        s, at = 1 + lax.div(t, CHUNKS), lax.rem(t, CHUNKS)
        for direction in range(2):
            c = at if direction == 0 else lax.rem(at + CHUNKS // 2, CHUNKS)
            ring(direction, s - 1, c, True).wait_recv()
            ring(direction, s, c, False).start()

    def ranks(i):
        at = i * piece
        here = pl.ds(at, piece)
        rev_col = cols_v[0, here, 0:1]
        hold_col = lax.shift_right_logical(rev_col, shift)
        before = (hold_col == hold_row) & (iota((piece, rows), 0) + at < iota((piece, rows), 1))
        rank_v[...] = rank_v[...] + jnp.sum(flag(before), axis=0, keepdims=True)
        lower = (rev_row >= lax.shift_left(hold_col, shift)) & (rev_row < rev_col)
        rank = jnp.sum(flag(lower), axis=1, keepdims=True).astype(I32)
        cols_v[3, here] = jnp.broadcast_to(rank, (piece, 8))

    def select(i):
        at = i * piece
        here = pl.ds(at, piece)
        rank = rank_v[0:1].astype(I32)
        high = jnp.where(rank >= half_cap, 1, 0)
        code = jnp.where(local_row, -1, hold_row * half_cap + rank + high * (slots - half_cap))
        at_slot = i * (2 * slots // PIECES)
        sel_v[pl.ds(at_slot, 2 * slots // PIECES)] = flag(
            iota((2 * slots // PIECES, rows), 0) + at_slot == code
        ).astype(BF16)
        rev_col = cols_v[0, here, 0:1]
        from_col = jnp.where(
            lax.shift_right_logical(rev_col, shift) == me_d, rev_col & (rows - 1), -1
        )
        loc_v[here] = flag(iota((piece, rows), 1) == from_col).astype(BF16)

    def receive(i, carry):
        here = pl.ds(i * piece, piece)
        hold_col = lax.shift_right_logical(cols_v[0, here, 0:1], shift)
        rank = cols_v[3, here, 0:1]
        high = jnp.where(rank >= half_cap, 1, 0)
        code = jnp.where(hold_col == me_d, -1, hold_col * half_cap + rank - high * half_cap)
        rec_v[here] = flag(iota((piece, slots), 1) == code).astype(BF16)
        keep_v[here] = flag((iota((piece, 128), 1) >= 64) == (high == 1))
        atom_piece = part_atoms // PIECES
        tgt_t[pl.ds(i * atom_piece, atom_piece)] = flag(
            iota((atom_piece, rows), 0) + i * atom_piece == ai_ref[1:2]
        ).astype(BF16)
        return carry

    def ends(i, carry):
        here = pl.ds(i * piece, piece)
        lanes = iota((piece, part_atoms), 1)
        src_g[here] = flag(lanes == cols_v[1, here, 0:1]).astype(BF16)
        tgt_g[here] = flag(lanes == cols_v[2, here, 0:1]).astype(BF16)
        return carry

    rank_v[...] = jnp.zeros_like(rank_v)
    middle = (steps - 2) * CHUNKS

    def first_turn(i, carry):
        if middle >= PIECES // 2:
            forward(i)
        ranks(2 * i)
        ranks(2 * i + 1)
        return carry

    def second_turn(i, carry):
        if middle >= 3 * PIECES // 2:
            forward(PIECES // 2 + i)
        select(i)
        return carry

    assert middle in (0, PIECES // 2, 3 * PIECES // 2)
    lax.fori_loop(0, PIECES // 2, first_turn, 0)
    lax.fori_loop(0, PIECES, second_turn, 0)

    arr_v[pl.ds(me_d * half_cap, half_cap)] = jnp.zeros((half_cap, 128), BF16)

    last = steps - 1
    split = CHUNKS // 2
    for j in range(CHUNKS):
        for direction in range(2):
            c = orders[direction][j]
            ring(direction, last - 1, c, True).wait_recv()
            if j < split:
                ring(direction, last, c, False).start()
    for j in range(split):
        for direction in range(2):
            ring(direction, last, orders[direction][j], True).wait_recv()

    others[0].wait()
    blocks = tiles_v.shape[0]
    lane_half = lax.shift_right_logical(iota((64, 128), 1), 6)
    for b in range(blocks):
        picked = []
        for k in range(2):
            source = ts_ref[k, b]
            owner = lax.shift_right_logical(source, log2(blocks))
            inner = source & (blocks - 1)
            value = gath[owner * groups + (inner & (groups - 1))]
            picked.append(
                jnp.where(lane_half == lax.shift_right_logical(inner, log2(groups)), value, jnp.zeros_like(value))
            )
        mixed = dot(tiles_v[b], jnp.concatenate(picked, axis=0))
        trip_v[pl.ds(b * 64, 64)] = (mixed + pltpu.roll(mixed, 64, 1)).astype(BF16)

    low_lanes = iota((slots, 128), 1) < 64
    pack_v[...] = jnp.where(
        low_lanes, dot(sel_v[pl.ds(0, slots)], trip_v[...]), dot(sel_v[pl.ds(slots, slots)], trip_v[...])
    ).astype(BF16)

    def send_dom(k, carry):
        peer = lax.rem(me_d + k, n_dom)
        pltpu.make_async_remote_copy(
            src_ref=pack_v.at[pl.ds(peer * half_cap, half_cap)],
            dst_ref=arr_v.at[pl.ds(me_d * half_cap, half_cap)],
            send_sem=x_sem.at[0],
            recv_sem=x_sem.at[1],
            device_id={"dom": peer},
            device_id_type=MESH,
        ).start()
        return carry

    lax.fori_loop(1, n_dom, send_dom, 0)
    all_but_one = pl.ds(0, slots - half_cap)
    exchange = pltpu.make_async_remote_copy(
        src_ref=pack_v.at[all_but_one],
        dst_ref=arr_v.at[all_but_one],
        send_sem=x_sem.at[0],
        recv_sem=x_sem.at[1],
        device_id={"dom": lax.rem(me_d + 1, n_dom)},
        device_id_type=MESH,
    )
    lax.fori_loop(0, PIECES, receive, 0)
    part = rows // 4
    for i in range(4):
        mir_v[pl.ds(i * part, part)] = dot(loc_v[pl.ds(i * part, part)], trip_v[...])
    for one in others[1:]:
        one.wait()
    exchange.wait()

    part = rows // 2

    def edge_part(i):
        here = pl.ds(i * part, part)
        found = dot(rec_v[here], arr_v[...]) * keep_v[here]
        mirrored = (found + pltpu.roll(found, 64, 1) + mir_v[here]).astype(BF16)
        both = jnp.where(iota((part, 128), 1) < 64, trip_v[here], mirrored)
        state = (edges_v[here].astype(F32) + dot(both, wup_v[...]) * ROOT_HALF).astype(BF16)
        middle = silu(dot(state, wres_v[0])).astype(BF16)
        branch = silu(dot(middle, wres_v[1]))
        state = ((state.astype(F32) + branch) * ROOT_HALF).astype(BF16)
        es_v[here] = state
        msg_v[here] = dot(state, wmsg_v[...]).astype(BF16)

    for i in range(2):
        edge_part(i)

    a_part = part_atoms // 4
    for i in range(4):
        here = pl.ds(i * a_part, a_part)
        rs_v[here] = dot(tgt_t[here], msg_v[...]).astype(BF16)

    def push(src, dst, sems, peer):
        pltpu.make_async_remote_copy(
            src_ref=src,
            dst_ref=dst,
            send_sem=z_sem.at[sems[0]],
            recv_sem=z_sem.at[sems[1]],
            device_id={"edge": peer},
            device_id_type=MESH,
        ).start()

    def local(ref, sems):
        return pltpu.make_async_remote_copy(
            src_ref=ref,
            dst_ref=ref,
            send_sem=z_sem.at[sems[0]],
            recv_sem=z_sem.at[sems[1]],
            device_id={"edge": right},
            device_id_type=MESH,
        )

    def away(d):
        return lax.rem(me_z + d + n_edge, n_edge)

    def atoms_of(device):
        return pl.ds(device * own_atoms, own_atoms)

    def slot_of(i):
        return pl.ds(i * own_atoms, own_atoms)

    hop = n_edge // 4
    half_own = own_atoms // 2

    def half_of(device, side):
        return pl.ds(device * own_atoms + side * half_own, half_own)

    for side in range(2):
        sign = 1 - 2 * side
        push(
            rs_v.at[half_of(away(sign * 2 * hop), side)],
            rel_v.at[half_of(side * hop + hop - 1, side)],
            (0, 1),
            away(sign * hop),
        )
    for d in range(2 * hop - 1, hop, -1):
        for side in range(2):
            sign = 1 - 2 * side
            push(
                rs_v.at[atoms_of(away(sign * d))],
                rel_v.at[slot_of(side * hop + d - hop - 1)],
                (0, 1),
                away(sign * (d - hop)),
            )
    for d in range(hop - 1, 0, -1):
        push(rs_v.at[atoms_of(away(d))], fin_v.at[slot_of(d - 1)], (0, 2), away(d))
        push(rs_v.at[atoms_of(away(-d))], fin_v.at[slot_of(hop + d - 1)], (0, 2), away(-d))
    for side in range(2):
        rel_v[half_of(side * hop + hop - 1, 1 - side)] = jnp.zeros((half_own, atom_width), BF16)
    lax.fori_loop(0, PIECES, ends, 0)

    def pre_part(i, carry):
        here = pl.ds(i * (rows // 4), rows // 4)
        pre_v[here] = dot(es_v[here], wjoin_v[pl.ds(2 * atom_width, width)])
        return carry

    local(rel_v.at[pl.ds(0, (2 * hop - 1) * own_atoms)], (0, 1)).wait_recv()
    for side in range(2):
        owner = away(hop if side == 0 else -hop)
        relayed = rs_v[atoms_of(owner)].astype(F32)
        for i in range(hop):
            relayed = relayed + rel_v[slot_of(side * hop + i)].astype(F32)
        hop_v[slot_of(side)] = relayed.astype(BF16)
        push(hop_v.at[slot_of(side)], fin_v.at[slot_of((side + 1) * hop - 1)], (0, 2), owner)
    lax.fori_loop(0, 4, pre_part, 0)
    local(fin_v, (0, 2)).wait_recv()
    own = atoms_of(me_z)
    total = rs_v[own].astype(F32)
    for i in range(2 * hop):
        total = total + fin_v[slot_of(i)].astype(F32)
    scaled = (total * EPA ** (-0.5)).astype(BF16)
    middle_atoms = silu(dot(scaled, watom_v[0])).astype(BF16)
    fresh = (atoms_ref[...].astype(F32) + dot(middle_atoms, watom_v[1])).astype(BF16)
    natoms_ref[...] = fresh
    na_v[own] = fresh

    for d in range(hop, 0, -1):
        push(na_v.at[own], na_v.at[own], (3, 4 if d == hop else 6), away(d))
        push(na_v.at[own], na_v.at[own], (3, 5 if d == hop else 6), away(-d))
    for side in range(2):
        sign = 1 - 2 * side
        passed = na_v.at[atoms_of(away(-sign * hop))]
        local(passed, (3, 4 + side)).wait_recv()
        far = na_v.at[half_of(away(-sign * hop), side)]
        push(far, far, (3, 6), away(sign * hop))
        for d in range(hop - 1, 0, -1):
            push(passed, passed, (3, 6), away(sign * d))
    local(na_v.at[pl.ds(0, (n_edge - 3) * own_atoms)], (3, 6)).wait_recv()

    most = pl.ds(0, part_atoms - own_atoms)
    local(rs_v.at[most], (0, 1)).wait_send()
    local(na_v.at[most], (3, 4)).wait_send()
    def drain(t, carry):
        s, c = lax.div(t, CHUNKS), lax.rem(t, CHUNKS)
        for direction in range(2):
            ring(direction, s, c, False).wait_send()
        return carry

    lax.fori_loop(0, last * CHUNKS, drain, 0)
    for j in range(split):
        for direction in range(2):
            ring(direction, last, orders[direction][j], False).wait_send()


def finish(fresh_ref, es_ref, pre_ref, na_ref, src_ref, tgt_ref, wjoin_ref, out_h, natoms_ref, out_v, sem):
    rows = es_ref.shape[0]
    part = rows // 4
    natoms_ref[...] = fresh_ref[...]
    copies = []
    for i in range(4):
        here = pl.ds(i * part, part)
        ends = jnp.concatenate([dot(src_ref[here], na_ref[...]), dot(tgt_ref[here], na_ref[...])], axis=1).astype(BF16)
        update = silu(dot(ends, wjoin_ref[pl.ds(0, 2 * na_ref.shape[1])]) + pre_ref[here])
        out_v[here] = ((es_ref[here].astype(F32) + update) * ROOT_HALF).astype(BF16)
        copies.append(pltpu.make_async_copy(out_v.at[here], out_h.at[here], sem.at[i]))
        copies[-1].start()
    for one in copies:
        one.wait()


def body(n_dom, n_edge, edges, atoms, reverse, atom_index, tile_source, tiles, weight_edge, weight_down, weight_up,
         weight_residual, weight_message, weight_atom, weight_join):
    rows, width = edges.shape
    own_atoms, atom_width = atoms.shape
    part_atoms = own_atoms * n_edge
    blocks = tiles.shape[0]
    channels = weight_down.shape[0]
    assert channels == 64 and tiles.shape[1:] == (64, 128)
    groups = blocks // 2
    capacity = rows // n_dom
    slots = n_dom * capacity // 2
    vmem = pl.BlockSpec(memory_space=pltpu.VMEM)
    hbm = pl.BlockSpec(memory_space=pltpu.HBM)
    fresh, state, pre, everyone, src_hot, tgt_hot, join = pl.pallas_call(
        functools.partial(kernel, n_dom, n_edge),
        out_shape=(
            jax.ShapeDtypeStruct((own_atoms, atom_width), BF16),
            jax.ShapeDtypeStruct((rows, width), BF16),
            jax.ShapeDtypeStruct((rows, width), F32),
            jax.ShapeDtypeStruct((part_atoms, atom_width), BF16),
            jax.ShapeDtypeStruct((rows, part_atoms), BF16),
            jax.ShapeDtypeStruct((rows, part_atoms), BF16),
            jax.ShapeDtypeStruct(weight_join.shape, BF16),
        ),
        in_specs=[hbm] * 13,
        out_specs=(vmem,) * 7,
        scratch_shapes=[
            pltpu.VMEM((rows, width), BF16),
            pltpu.VMEM(tiles.shape, BF16),
            pltpu.VMEM(weight_edge.shape, BF16),
            pltpu.VMEM((2 * channels, width), BF16),
            pltpu.VMEM((2, width, width), BF16),
            pltpu.VMEM(weight_message.shape, BF16),
            pltpu.VMEM(weight_atom.shape, BF16),
            pltpu.SMEM(tile_source.shape[::-1], I32),
            pltpu.VMEM((1, rows), I32),
            pltpu.VMEM((2, rows), I32),
            pltpu.VMEM((own_atoms, atom_width), BF16),
            pltpu.VMEM(weight_down.shape, BF16),
            pltpu.VMEM((n_edge * groups, 64, 128), BF16),
            pltpu.VMEM((rows, 128), BF16),
            pltpu.VMEM((slots, 128), BF16),
            pltpu.VMEM((slots, 128), BF16),
            pltpu.VMEM((rows, 128), F32),
            pltpu.VMEM((2 * slots, rows), BF16),
            pltpu.VMEM((rows, rows), BF16),
            pltpu.VMEM((rows, slots), BF16),
            pltpu.VMEM((rows, 128), F32),
            pltpu.VMEM((part_atoms, rows), BF16),
            pltpu.VMEM((4, rows, 8), I32),
            pltpu.VMEM((8, rows), F32),
            pltpu.VMEM((rows, atom_width), BF16),
            pltpu.VMEM((part_atoms, atom_width), BF16),
            pltpu.VMEM((part_atoms // 2, atom_width), BF16),
            pltpu.VMEM((2 * own_atoms, atom_width), BF16),
            pltpu.VMEM((part_atoms // 2, atom_width), BF16),
            pltpu.SemaphoreType.DMA((2 * CHUNKS + 12,)),
            pltpu.SemaphoreType.DMA((2, n_edge // 2, CHUNKS)),
            pltpu.SemaphoreType.DMA((2, n_edge // 2, CHUNKS)),
            pltpu.SemaphoreType.DMA((2,)),
            pltpu.SemaphoreType.DMA((7,)),
        ],
        compiler_params=pltpu.CompilerParams(
            collective_id=0, has_side_effects=True, vmem_limit_bytes=34 * 1024 * 1024
        ),
    )(
        *(
            pltpu.with_memory_space_constraint(one, pltpu.HBM)
            for one in (
                tile_source.T,
                reverse.reshape(1, rows),
                atom_index,
                atoms,
                weight_down,
                edges,
                tiles,
                weight_edge,
                weight_up.reshape(2 * channels, width),
                weight_residual.reshape(2, width, width),
                weight_message,
                weight_atom,
                weight_join,
            )
        ),
    )
    return pl.pallas_call(
        finish,
        out_shape=(
            jax.ShapeDtypeStruct((rows, width), BF16),
            jax.ShapeDtypeStruct((own_atoms, atom_width), BF16),
        ),
        in_specs=[vmem] * 7,
        out_specs=(hbm, vmem),
        scratch_shapes=[pltpu.VMEM((rows, width), BF16), pltpu.SemaphoreType.DMA((4,))],
        compiler_params=pltpu.CompilerParams(vmem_limit_bytes=12 * 1024 * 1024),
    )(fresh, state, pre, everyone, src_hot, tgt_hot, join)


def solution(mesh):
    n_dom, n_edge = mesh.shape["dom"], mesh.shape["edge"]
    placed = (
        P(("dom", "edge"), None),
        P(("dom", "edge"), None),
        P(("dom", "edge")),
        P(None, ("dom", "edge")),
        P(("dom", "edge"), None),
        P(("dom", "edge"), None, None),
        P(),
        P(),
        P(),
        P(),
        P(),
        P(),
        P(),
    )
    return jax.shard_map(
        functools.partial(body, n_dom, n_edge),
        mesh=mesh,
        in_specs=placed,
        out_specs=(P(("dom", "edge"), None), P(("dom", "edge"), None)),
        check_vma=False,
    )
```
